256 devices in a mesh: gx: 8 (over x, core), gy: 32 (over z, y).
Axes of the slice: x: 4, y: 4, z: 8, core: 2. Of those that a mesh axis runs over, the one named last changes fastest.
Arguments:
- populations: float32 [19, 32, 256, 128], P(None, 'gx', 'gy'), as said below
- wall_speed: float32 [3, 16384], P(None, ('gx', 'gy')), may hold values from -0.15 to 0.15
- adjoint_seed: float32 [19, 32, 256, 128], P(None, 'gx', 'gy'), may hold values from -6 to 6
- link_cell: int32 [4, 262144], P(None, ('gx', 'gy')), may hold values from 0 to 4095, as said below
- link_dir: int32 [4, 262144], P(None, ('gx', 'gy')), may hold values from 1 to 18
- link_node: int32 [4, 262144], P(None, ('gx', 'gy')), may hold values from 0 to 16383, as said below
- live_links: int32 [4, 256], P(None, ('gx', 'gy')), may hold values from 256 to 1024
- node_slot: int32 [16384], replicated, may hold values from 0 to 16383, as said below
Outputs:
- adjoint_start: float32 [19, 32, 256, 128], P(None, 'gx', 'gy')
- wall_gradient: float32 [3, 16384], P(None, ('gx', 'gy'))
The draws below stay inside these ranges and needn't reach their ends.
Inputs may be any that keep to these rules, and one draw needn't show every extreme that they name: `link_cell`: A link's cell is numbered x slowest and z fastest within its device's brick of 4 x 8 x 128 cells. `link_node`: A link's node has its slot among the 2048 slots of the devices with the same gx index as the link's device. `node_slot`: A permutation; slot s is held by device s // 64 of gx+gy. `populations`: every population is positive.
All inputs are finite; a program needn't handle non-finite values.
Results may differ from the reference program's by a relative error of at most 0.0003.
Values sent between devices are 32-bit elements; how exact they have to be, the bound alone decides.
No kernel may reach another device: no remote copies, remote signals or barrier semaphores. Data moves between devices by JAX's collectives and lax.ppermute only.
A program may use at most 64 MiB of HBM per device.

```python
import jax
import jax.numpy as jnp
from jax import lax

CX = 4
CY = 8
NZ = 128
STEPS = 4
NX = 32
NY = 256
CELLS_DEV = 4096
LINKS_DEV = 1024
LINKS = 262144
NODES = 16384
COLUMN_NODES = 2048
N_GY = 32
DEVICES = 256


WEIGHTS = [1.0 / 3.0] + [1.0 / 18.0] * 6 + [1.0 / 36.0] * 12


def draw_populations(key, part):
    weight = jnp.array(WEIGHTS, dtype=jnp.float32).reshape(19, 1, 1, 1)
    noise = jnp.clip(0.1 * jax.random.normal(key, (19, NX, NY, NZ), jnp.float32), -0.3, 0.3)
    return weight * (1.0 + noise)


def link_layout(key):
    key_cell, key_dir, key_pick, key_perm = jax.random.split(jax.random.fold_in(key, 7), 4)
    cells = jax.random.randint(key_cell, (STEPS, LINKS), 0, CELLS_DEV, jnp.int32)
    dirs = jax.random.randint(key_dir, (STEPS, LINKS), 1, 19, jnp.int32)
    slots = jax.random.permutation(key_perm, NODES).astype(jnp.int32)
    owners = jnp.argsort(slots, stable=True).astype(jnp.int32)
    positions = jnp.arange(LINKS, dtype=jnp.int32)
    column = positions // LINKS_DEV // N_GY
    offset = jax.random.randint(key_pick, (STEPS, LINKS), 0, COLUMN_NODES, jnp.int32)
    chosen = column[None, :] * COLUMN_NODES + offset
    nodes = owners[chosen]
    return (cells, dirs, nodes, slots)


def draw_link_cell(key, part):
    return link_layout(key)[0]


def draw_link_dir(key, part):
    return link_layout(key)[1]


def draw_link_node(key, part):
    return link_layout(key)[2]


def draw_node_slot(key, part):
    return link_layout(key)[3]


def draw_live_links(key, part):
    key_count, key_pick = jax.random.split(jax.random.fold_in(key, 13))
    counts = jax.random.randint(key_count, (STEPS, DEVICES), LINKS_DEV // 4, LINKS_DEV + 1, jnp.int32)
    pick = jax.random.randint(key_pick, (STEPS, 1), 0, DEVICES, jnp.int32)
    spots = jnp.arange(DEVICES, dtype=jnp.int32)[None, :]
    counts = jnp.where(spots == pick, LINKS_DEV, counts)
    counts = jnp.where(spots == (pick + 1) % DEVICES, LINKS_DEV // 4, counts)
    return counts


def block_scale(key, shape, cuts, least, largest):
    level = 1.0
    for dim, parts in cuts:
        steps = jax.random.uniform(jax.random.fold_in(jax.random.fold_in(key, 6), dim), (parts,), jnp.float32, least / len(cuts), largest / len(cuts))
        level = level * jnp.repeat(jnp.exp(steps), shape[dim] // parts).reshape((-1,) + (1,) * (len(shape) - 1 - dim))
    return level


def centred(key, shape, width, most, shards=(), held_as=jnp.bfloat16):
    gain = block_scale(key, shape, shards, -0.22, 0.18) if shards else 1.0
    values = jax.random.normal(key, shape, jnp.float32) * width * gain
    return jnp.minimum(jnp.maximum(values, -most), most).astype(held_as)


def setup_inputs(seed: int = 0) -> dict:
    splits = jax.random.split(jax.random.key(seed), 9)
    populations = draw_populations(jax.random.fold_in(splits[8], 71), 0)
    wall_speed = jnp.clip(jax.random.uniform(splits[1], (3, NODES), jnp.float32, -0.15, 0.15) * block_scale(splits[1], (3, NODES), ((1, 256),), -0.4, 0.0), -0.15, 0.15)
    adjoint_seed = centred(splits[2], (19, NX, NY, NZ), 1.0, 6.0, ((1, 8), (2, 32)), jnp.float32)
    link_cell = draw_link_cell(jax.random.fold_in(splits[8], 71), 0)
    link_dir = draw_link_dir(jax.random.fold_in(splits[8], 71), 0)
    link_node = draw_link_node(jax.random.fold_in(splits[8], 71), 0)
    live_links = draw_live_links(jax.random.fold_in(splits[8], 71), 0)
    node_slot = draw_node_slot(jax.random.fold_in(splits[8], 71), 0)
    return {"populations": populations, "wall_speed": wall_speed, "adjoint_seed": adjoint_seed, "link_cell": link_cell, "link_dir": link_dir, "link_node": link_node, "live_links": live_links, "node_slot": node_slot}


VELOCITIES = [(0, 0, 0), (1, 0, 0), (-1, 0, 0), (0, 1, 0), (0, -1, 0), (0, 0, 1), (0, 0, -1), (1, 1, 0), (-1, -1, 0), (1, -1, 0), (-1, 1, 0), (1, 0, 1), (-1, 0, -1), (1, 0, -1), (-1, 0, 1), (0, 1, 1), (0, -1, -1), (0, 1, -1), (0, -1, 1)]
WEIGHTS = [1.0 / 3.0] + [1.0 / 18.0] * 6 + [1.0 / 36.0] * 12
OMEGA = 1.6
KAPPA = 0.5

def velocity_table(component, dtype):
    return jnp.array([float(vel[component]) for vel in VELOCITIES], dtype=dtype)

def collide(pops):
    dtype = pops.dtype
    shape = (19,) + (1,) * (pops.ndim - 1)
    vel_x = velocity_table(0, dtype).reshape(shape)
    vel_y = velocity_table(1, dtype).reshape(shape)
    vel_z = velocity_table(2, dtype).reshape(shape)
    weight = jnp.array(WEIGHTS, dtype=dtype).reshape(shape)
    density = lax.optimization_barrier(jnp.sum(pops, axis=0))
    speed_x = lax.optimization_barrier(jnp.sum(vel_x * pops, axis=0)) / density
    speed_y = lax.optimization_barrier(jnp.sum(vel_y * pops, axis=0)) / density
    speed_z = lax.optimization_barrier(jnp.sum(vel_z * pops, axis=0)) / density
    along = vel_x * speed_x + vel_y * speed_y + vel_z * speed_z
    square = speed_x * speed_x + speed_y * speed_y + speed_z * speed_z
    equilibrium = weight * density * (1.0 + 3.0 * along + 4.5 * along * along - 1.5 * square)
    return (pops - OMEGA * (pops - equilibrium), density)

def link_terms(relaxed_flat, density_flat, flat_cell, dirs, ulink, live):
    dtype = relaxed_flat.dtype
    opposite = dirs + 1 - 2 * ((dirs + 1) % 2)
    onehot = (dirs[:, None] == jnp.arange(19, dtype=jnp.int32)[None, :]).astype(dtype)
    weight = lax.optimization_barrier(jnp.sum(onehot * jnp.array(WEIGHTS, dtype=dtype)[None, :], axis=1))
    push = jnp.zeros(dirs.shape, dtype)
    for component in range(3):
        link_vel = lax.optimization_barrier(jnp.sum(onehot * velocity_table(component, dtype)[None, :], axis=1))
        push = push + link_vel * ulink[component]
    forward_pop = relaxed_flat[dirs, flat_cell]
    backward_pop = relaxed_flat[opposite, flat_cell]
    delta = (KAPPA * (forward_pop - backward_pop) - 6.0 * weight * density_flat[flat_cell] * push) * live
    return (opposite, delta)

def one_step(pops, wall_speed, cells, dirs, nodes, counts, node_slot):
    dtype = pops.dtype
    relaxed, density = collide(pops)
    read = jnp.stack([jnp.roll(relaxed[lane], VELOCITIES[lane], axis=(0, 1, 2)) for lane in range(19)])
    positions = jnp.arange(LINKS, dtype=jnp.int32)
    device = positions // LINKS_DEV
    col_x = device // N_GY
    col_y = device % N_GY
    live = (positions % LINKS_DEV < counts[device]).astype(dtype)
    local_x = cells // (CY * NZ)
    local_y = cells // NZ % CY
    local_z = cells % NZ
    flat_cell = (((col_x * CX + local_x) * NY + col_y * CY + local_y) * NZ + local_z).astype(jnp.int32)
    ulink = wall_speed[:, node_slot[nodes]]
    relaxed_flat = relaxed.reshape(19, -1)
    density_flat = density.reshape(-1)
    opposite, delta = link_terms(relaxed_flat, density_flat, flat_cell, dirs, ulink, live)
    result = read.reshape(19, -1).at[opposite, flat_cell].add(delta)
    return result.reshape(pops.shape)

def reference(populations, wall_speed, adjoint_seed, link_cell, link_dir, link_node, live_links, node_slot):
    states = [populations]
    for moment in range(STEPS - 1):
        states.append(one_step(states[-1], wall_speed, link_cell[moment], link_dir[moment], link_node[moment], live_links[moment], node_slot))
    adjoint = adjoint_seed
    wall_gradient = jnp.zeros_like(wall_speed)
    for moment in reversed(range(STEPS)):

        def stepper(pops, speeds, moment=moment):
            return one_step(pops, speeds, link_cell[moment], link_dir[moment], link_node[moment], live_links[moment], node_slot)
        unused, pullback = jax.vjp(stepper, states[moment], wall_speed)
        adjoint, speed_part = pullback(adjoint)
        wall_gradient = wall_gradient + speed_part
    return (adjoint, wall_gradient)
```

```python
import jax
import jax.numpy as jnp
from jax import lax
from jax.experimental import pallas as pl
from jax.experimental.pallas import tpu as pltpu
from jax.sharding import PartitionSpec as P

VELOCITIES = [
    (0, 0, 0),
    (1, 0, 0),
    (-1, 0, 0),
    (0, 1, 0),
    (0, -1, 0),
    (0, 0, 1),
    (0, 0, -1),
    (1, 1, 0),
    (-1, -1, 0),
    (1, -1, 0),
    (-1, 1, 0),
    (1, 0, 1),
    (-1, 0, -1),
    (1, 0, -1),
    (-1, 0, 1),
    (0, 1, 1),
    (0, -1, -1),
    (0, 1, -1),
    (0, -1, 1),
]
WEIGHTS = [1.0 / 3.0] + [1.0 / 18.0] * 6 + [1.0 / 36.0] * 12
OPPOSITE = [0] + [q + 1 if q % 2 else q - 1 for q in range(1, 19)]
OMEGA = 1.6
F32 = jnp.float32
BF16 = jnp.bfloat16
EXACT = lax.Precision.HIGHEST

POP_TILES = 152
SEED_TILES = 76
LIST_TILES = 8
X_TILES = POP_TILES + SEED_TILES + 3 * LIST_TILES
Y_TILES = 38 + 19 + LIST_TILES


def full(shape=None):
    return pl.BlockSpec(memory_space=pltpu.VMEM)


def row_iota(shape):
    return lax.broadcasted_iota(jnp.int32, shape, 0)


def signs(dirs, component):
    out = jnp.zeros(dirs.shape, F32)
    for q in range(1, 19):
        c = VELOCITIES[q][component]
        if c:
            out = jnp.where(dirs == q, float(c), out)
    return out


def low_half(shape):
    return lax.broadcasted_iota(jnp.int32, shape, len(shape) - 2) < 4


def prep_kernel(
    base, pops, seed, wall, cell, dirs, node, live, table, up_msg, down_msg, lists, slots
):
    low = low_half((8, 128))
    pair = row_iota((8, 128)) // 2
    for q in range(19):
        for i in range(2):
            even = pops[q, 2 * i]
            odd = pltpu.roll(pops[q, 2 * i + 1], 4, 0)
            down_msg[2 * q + i] = jnp.where(low, even, odd)
            up_msg[2 * q + i] = jnp.where(low, odd, even)
        down = seed[q, 0]
        up = pltpu.roll(seed[q, 0], 2, 0)
        for x in range(1, 4):
            down = jnp.where(pair == x, pltpu.roll(seed[q, x], 2 * x, 0), down)
            up = jnp.where(pair == x, pltpu.roll(seed[q, x], (2 * x + 2) % 8, 0) if x < 3 else seed[q, x], up)
        down_msg[38 + q] = down
        up_msg[38 + q] = up
    slot_table = table[...]
    high = (slot_table // 128).astype(F32).astype(BF16)
    rest = (slot_table % 128).astype(F32).astype(BF16)
    both = jnp.concatenate([high, rest], axis=0)
    lanes = row_iota((128, 1024))
    lane = lax.broadcasted_iota(jnp.int32, (1, 1024), 1)
    codes, pushes = [], []
    for s in range(4):
        nodes = node[s : s + 1, :]
        hot = jnp.where(lanes == nodes % 128, 1.0, 0.0).astype(BF16)
        picked = jnp.dot(both, hot, preferred_element_type=F32)
        match = lanes == nodes // 128
        slot_high = jnp.sum(jnp.where(match, picked[:128], 0.0), axis=0, keepdims=True)
        slot_rest = jnp.sum(jnp.where(match, picked[128:], 0.0), axis=0, keepdims=True)
        slot = (slot_high * 128.0 + slot_rest).astype(jnp.int32) - base[0]
        slots[s : s + 1, :] = slot
        owner = row_iota((32, 1024)) == slot // 64
        place = jnp.where(row_iota((64, 1024)) == slot % 64, 1.0, 0.0)
        direction = dirs[s : s + 1, :]
        push = jnp.zeros((1, 1024), F32)
        for c in range(3):
            speeds = jnp.dot(
                wall[:, 64 * c : 64 * c + 64], place, precision=EXACT, preferred_element_type=F32
            )
            speed = jnp.sum(jnp.where(owner, speeds, 0.0), axis=0, keepdims=True)
            push = push + signs(direction, c) * speed
        opposite = direction + 1 - 2 * ((direction + 1) % 2)
        code = opposite * 4096 + cell[s : s + 1, :]
        codes.append(jnp.where(lane < live[s : s + 1, :], code, -1).astype(F32))
        pushes.append(push)
    table8 = jnp.concatenate(codes + pushes, axis=0)
    lists[...] = table8
    for t in range(8):
        up_msg[57 + t] = table8[:, 128 * t : 128 * t + 128]
        down_msg[57 + t] = table8[:, 128 * t : 128 * t + 128]


def pack_kernel(pops, seed, from_up, from_down, lists, right_msg, left_msg):
    low = low_half((8, 128))
    sub = row_iota((8, 128))
    for q in range(19):
        for i in range(2):
            up = from_up[2 * q + i]
            down = from_down[2 * q + i]
            even = jnp.where(low, up, down)
            odd = pltpu.roll(jnp.where(low, down, up), 4, 0)
            for x, halo in ((2 * i, even), (2 * i + 1, odd)):
                k = (q * 4 + x) * 2
                own = pops[q, x]
                for msg in (right_msg, left_msg):
                    msg[k] = own
                    msg[k + 1] = halo
        up = from_up[38 + q]
        down = from_down[38 + q]
        for x in range(4):
            halo = widen_two(up, down, x, sub)
            msg = left_msg if x < 2 else right_msg
            k = POP_TILES + (q * 2 + x % 2) * 2
            msg[k] = seed[q, x]
            msg[k + 1] = halo
    k = POP_TILES + SEED_TILES
    for t in range(8):
        for msg in (right_msg, left_msg):
            msg[k + t] = lists[:, 128 * t : 128 * t + 128]
            msg[k + 8 + t] = from_up[57 + t]
            msg[k + 16 + t] = from_down[57 + t]


def widen_two(up, down, x, sub):
    first = up if x == 0 else pltpu.roll(up, 8 - 2 * x, 0)
    last = down if x == 3 else pltpu.roll(down, 6 - 2 * x, 0)
    return jnp.where(sub < 4, first, last)


def onehot(code, rows, iota):
    out = []
    padded = (rows + 15) // 16 * 16
    for start in range(0, padded, 256):
        count = min(256, padded - start)
        wanted = jnp.clip(code - float(start), -1.0, 256.0).astype(BF16)
        out.append(
            jnp.concatenate(
                [
                    jnp.where(
                        iota[:count] == wanted[:, 128 * t : 128 * t + 128],
                        jnp.array(1.0, BF16),
                        jnp.array(0.0, BF16),
                    )
                    for t in range(8)
                ],
                axis=1,
            )
        )
    return out[0] if len(out) == 1 else jnp.concatenate(out, axis=0)


def iota256():
    return row_iota((256, 128)).astype(F32).astype(BF16)


def split_code(code):
    number = code.astype(jnp.int32)
    dead = number < 0
    z = jnp.where(dead, -1, number % 128)
    row = jnp.where(dead, 0, number // 128)
    return dead, row // 32 - 1, (row // 8) % 4, row % 8, z


def scatter_table(code, push, first, count, iota, part):
    dead, lane_q, x, y, z = split_code(code)
    index = lane_q * count + (x - first)
    outside = dead | (x < first) | (x >= first + count)
    if part == "all":
        row, rows = index * 8 + y, 144 * count
    elif part == "low":
        row, rows = index * 4 + y, 72 * count
        outside = outside | (y >= 4)
    else:
        row, rows = (index + 1 - 2 * (index % 2)) * 4 + y - 4, 72 * count
        outside = outside | (y < 4)
    target = onehot(jnp.where(outside, -1, row).astype(F32), rows, iota)
    zcode = z.astype(F32).astype(BF16)
    high = push.astype(BF16)
    mid = (push - high.astype(F32)).astype(BF16)
    last = (push - high.astype(F32) - mid.astype(F32)).astype(BF16)
    zero = jnp.array(0.0, BF16)
    blocks = [[], [], [], []]
    for t in range(8):
        cut = slice(128 * t, 128 * t + 128)
        match = iota[:128] == zcode[:, cut]
        blocks[0].append(jnp.where(match, jnp.array(1.0, BF16), zero))
        for b, piece in zip(blocks[1:], (high, mid, last)):
            b.append(jnp.where(match, piece[:, cut], zero))
    values = jnp.concatenate([jnp.concatenate(b, axis=1) for b in blocks], axis=0)
    dense = lax.dot_general(
        target, values, (((1,), (1,)), ((), ())), preferred_element_type=F32
    )[:rows]
    return dense[:, :128], dense[:, 128:256] + dense[:, 256:384] + dense[:, 384:]


def scatter_columns(lists, s, first, count, iota, n_ref, s_ref, where):
    own, up, down = lists
    n, p = scatter_table(own[s : s + 1, :], own[4 + s : 5 + s, :], first, count, iota, "all")
    at = pl.ds(where, count)
    n_ref[s, :, at, 0:8, :] = n.reshape(18, count, 8, 128)
    s_ref[s, :, at, 0:8, :] = p.reshape(18, count, 8, 128)
    above = scatter_table(up[s : s + 1, :], up[4 + s : 5 + s, :], first, count, iota, "low")
    below = scatter_table(down[s : s + 1, :], down[4 + s : 5 + s, :], first, count, iota, "high")
    shape = (9 * count, 8, 128)
    low = low_half(shape)
    for ref, a, b in zip((n_ref, s_ref), above, below):
        a, b = a.reshape(shape), b.reshape(shape)
        even = jnp.where(low, a, b)
        odd = pltpu.roll(jnp.where(low, b, a), 4, 1)
        halo = jnp.stack([even, odd], axis=1).reshape(18, count, 8, 128)
        ref[s, :, at, 8:16, :] = halo


def read_list(ref, start):
    return jnp.concatenate([ref[start + t] for t in range(8)], axis=1)


def own_links_kernel(lists, from_up, from_down, n_ref, s_ref):
    iota = iota256()
    both = (lists[...], read_list(from_up, 57), read_list(from_down, 57))
    for s in range(4):
        scatter_columns(both, s, 0, 4, iota, n_ref, s_ref, 0)


def shifted(value, cy, cz):
    if cy:
        value = pltpu.roll(value, cy % 16, 0)
    if cz:
        value = pltpu.roll(value, cz % 128, 1)
    return value


def moments(f):
    rho = f[0]
    for q in range(1, 19):
        rho = rho + f[q]
    inverse = 1.0 / rho
    speeds = []
    for c in range(3):
        total = None
        for q in range(1, 19):
            v = VELOCITIES[q][c]
            if v:
                total = (f[q] if v > 0 else -f[q]) if total is None else (total + f[q] if v > 0 else total - f[q])
        speeds.append(total * inverse)
    return rho, speeds


def along(speeds, q):
    total = None
    for c in range(3):
        v = VELOCITIES[q][c]
        if v:
            term = speeds[c] if v > 0 else -speeds[c]
            total = term if total is None else total + term
    return total


def collide_column(f):
    rho, speeds = moments(f)
    rest = 1.0 - 1.5 * (speeds[0] * speeds[0] + speeds[1] * speeds[1] + speeds[2] * speeds[2])
    out = [(1.0 - OMEGA) * f[0] + (OMEGA * WEIGHTS[0]) * rho * rest]
    for q in range(1, 19, 2):
        cu = along(speeds, q)
        scale = (OMEGA * WEIGHTS[q]) * rho
        even = scale * (rest + 4.5 * cu * cu)
        odd = scale * (3.0 * cu)
        out.append((1.0 - OMEGA) * f[q] + (even + odd))
        out.append((1.0 - OMEGA) * f[q + 1] + (even - odd))
    return out, rho


def collide_into(load, start, count, relaxed, density):
    def body(i, carry):
        f = [load(q, i) for q in range(19)]
        g, rho = collide_column(f)
        for q in range(19):
            relaxed[q, start + i] = g[q]
        density[start + i] = rho
        return carry

    lax.fori_loop(0, count, body, 0)


def stream_into(relaxed, density, n_ref, s_ref, s, start, count, out, out_shift):
    def body(i, carry):
        x = start + i
        rho = density[x]
        out[0, x - out_shift] = relaxed[0, x]
        for q in range(1, 19):
            p = OPPOSITE[q]
            cx, cy, cz = VELOCITIES[q]
            moved = shifted(relaxed[q, x - cx], cy, cz)
            bounce = (0.5 * n_ref[s, q - 1, x]) * (relaxed[p, x] - relaxed[q, x])
            push = (6.0 * WEIGHTS[q]) * rho * s_ref[s, q - 1, x]
            out[q, x - out_shift] = moved + (bounce - push)
        return carry

    lax.fori_loop(0, count, body, 0)


def adjoint_column(f, arrived, local, counts, pushes):
    rho, speeds = moments(f)
    b = [arrived[0]]
    direct = None
    for q in range(1, 19):
        p = OPPOSITE[q]
        b.append(
            arrived[q] + 0.5 * (counts[p - 1] * local[p] - counts[q - 1] * local[q])
        )
        term = (6.0 * WEIGHTS[q]) * (pushes[q - 1] * local[q])
        direct = term if direct is None else direct + term
    beta = [WEIGHTS[q] * b[q] for q in range(19)]
    total = beta[0]
    first = [None] * 3
    second = [None] * 3
    for q in range(1, 19, 2):
        plus = beta[q] + beta[q + 1]
        minus = beta[q] - beta[q + 1]
        total = total + plus
        inner = along(speeds, q) * plus
        for c in range(3):
            v = VELOCITIES[q][c]
            if v:
                m = minus if v > 0 else -minus
                k = inner if v > 0 else -inner
                first[c] = m if first[c] is None else first[c] + m
                second[c] = k if second[c] is None else second[c] + k
    square = speeds[0] * speeds[0] + speeds[1] * speeds[1] + speeds[2] * speeds[2]
    curved = speeds[0] * second[0] + speeds[1] * second[1] + speeds[2] * second[2]
    rest = OMEGA * (total - 4.5 * curved + 1.5 * square * total) - direct
    slopes = [
        OMEGA * (3.0 * first[c] + 9.0 * second[c] - 3.0 * speeds[c] * total) for c in range(3)
    ]
    out = [(1.0 - OMEGA) * b[0] + rest]
    for q in range(1, 19, 2):
        cu = along(slopes, q)
        out.append((1.0 - OMEGA) * b[q] + (rest + cu))
        out.append((1.0 - OMEGA) * b[q + 1] + (rest - cu))
    return out, rho


def adjoint_at(load_f, adjoint, x, counts, pushes):
    f = [load_f(q) for q in range(19)]
    local = [adjoint(q, x) for q in range(19)]
    arrived = []
    for q in range(19):
        cx, cy, cz = VELOCITIES[q]
        value = adjoint(q, x + cx) if cx else local[q]
        arrived.append(shifted(value, -cy, -cz))
    out, rho = adjoint_column(
        f, arrived, local, [counts(q) for q in range(18)], [pushes(q) for q in range(18)]
    )
    return out, rho, local


def ext(ref, k):
    return jnp.concatenate([ref[k], ref[k + 1]], axis=0)


def window_kernel(
    right_msg,
    left_msg,
    from_left,
    from_right,
    n_own,
    s_own,
    f1_out,
    n1_out,
    s1_out,
    a2_out,
    up_msg,
    down_msg,
    pull,
    counts,
    pushes,
    relaxed,
    density,
    f2,
    f3,
    a4,
    a3,
    sems,
):
    copies = [
        pltpu.make_async_copy(n_own, counts.at[:, :, 4:8], sems.at[0]),
        pltpu.make_async_copy(s_own, pushes.at[:, :, 4:8], sems.at[1]),
    ]
    for copy in copies:
        copy.start()
    for ref, start in ((from_left, 0), (right_msg, 4), (from_right, 8)):

        def load(q, i, ref=ref):
            return ref[pl.ds((q * 4 + i) * 2, 2)].reshape(16, 128)

        collide_into(load, start, 4, relaxed, density)
    iota = iota256()
    k = POP_TILES + SEED_TILES
    for ref, right in ((from_left, False), (from_right, True)):
        lists = [read_list(ref, k + 8 * i) for i in range(3)]
        for s, count in ((0, 3), (1, 2), (2, 1), (3, 1)):
            first = 0 if right else 4 - count
            where = 8 if right else 4 - count
            scatter_columns(lists, s, first, count, iota, counts, pushes, where)
    for copy in copies:
        copy.wait()
    stream_into(relaxed, density, counts, pushes, 0, 1, 10, f2, 0)
    for q in range(19):
        f1_out[q] = f2[q, 3:9]
    n1_out[...] = counts[1, :, 3:9]
    s1_out[...] = pushes[1, :, 3:9]
    collide_into(lambda q, i: f2[q, 1 + i], 1, 10, relaxed, density)
    stream_into(relaxed, density, counts, pushes, 1, 2, 8, f2, 0)
    collide_into(lambda q, i: f2[q, 2 + i], 2, 8, relaxed, density)
    stream_into(relaxed, density, counts, pushes, 2, 3, 6, f3, 0)
    for q in range(19):
        for x in range(2):
            k = POP_TILES + (q * 2 + x) * 2
            a4[q, 2 + x] = ext(from_left, k)
            a4[q, 4 + x] = ext(left_msg, k)
            a4[q, 6 + x] = ext(right_msg, k)
            a4[q, 8 + x] = ext(from_right, k)

    def third(i, carry):
        x = 3 + i
        out, rho, local = adjoint_at(
            lambda q: f3[q, x],
            lambda q, at: a4[q, at],
            x,
            lambda q: counts[3, q, x],
            lambda q: pushes[3, q, x],
        )
        for q in range(19):
            a3[q, x] = out[q]

        @pl.when((x >= 4) & (x < 8))
        def _():
            for q in range(1, 19):
                pull[0, q - 1, x - 4] = ((-6.0 * WEIGHTS[q]) * rho * local[q])[:8]

        return carry

    lax.fori_loop(0, 6, third, 0)

    def second(i, carry):
        x = 4 + i
        out, rho, local = adjoint_at(
            lambda q: f2[q, x],
            lambda q, at: a3[q, at],
            x,
            lambda q: counts[2, q, x],
            lambda q: pushes[2, q, x],
        )
        for q in range(19):
            a2_out[q, i] = out[q][:8]
        for q in range(1, 19):
            pull[1, q - 1, i] = ((-6.0 * WEIGHTS[q]) * rho * local[q])[:8]
        return carry

    lax.fori_loop(0, 4, second, 0)
    pair = row_iota((8, 128)) // 2
    for q in range(19):
        down = a2_out[q, 0]
        up = pltpu.roll(a2_out[q, 0], 2, 0)
        for x in range(1, 4):
            value = a2_out[q, x]
            down = jnp.where(pair == x, pltpu.roll(value, 2 * x, 0), down)
            up = jnp.where(pair == x, pltpu.roll(value, (2 * x + 2) % 8, 0) if x < 3 else value, up)
        down_msg[q] = down
        up_msg[q] = up


def pack_adjoint_kernel(a2, from_up, from_down, right_msg, left_msg):
    sub = row_iota((8, 128))
    for q in range(19):
        for x in range(4):
            msg = left_msg if x < 2 else right_msg
            k = (q * 2 + x % 2) * 2
            msg[k] = a2[q, x]
            msg[k + 1] = widen_two(from_up[q], from_down[q], x, sub)


def link_gradient(pulls, lists, slots, dirs, steps):
    iota = iota256()
    total = jnp.zeros((32, 192), F32)
    lanes = row_iota((128, 1024))
    for i, s in enumerate(steps):
        code = lists[s : s + 1, :]
        dead, lane_q, x, y, z = split_code(code)
        row = jnp.where(dead, -1, lane_q * 32 + x * 8 + y).astype(F32)
        hot = onehot(row, 576, iota)
        high = pulls[i].astype(BF16)
        rest = (pulls[i] - high.astype(F32)).astype(BF16)
        low = (pulls[i] - high.astype(F32) - rest.astype(F32)).astype(BF16)
        picked = lax.dot_general(
            jnp.concatenate([high, rest, low], axis=1),
            hot,
            (((0,), (0,)), ((), ())),
            preferred_element_type=F32,
        )
        match = lanes == z
        value = jnp.sum(
            jnp.where(match, picked[:128] + picked[128:256] + picked[256:], 0.0),
            axis=0,
            keepdims=True,
        )
        slot = slots[s : s + 1, :]
        direction = dirs[s : s + 1, :]
        owner = jnp.where(row_iota((32, 1024)) == slot // 64, 1.0, 0.0)
        place = row_iota((64, 1024)) == slot % 64
        parts = jnp.concatenate(
            [jnp.where(place, value * signs(direction, c), 0.0) for c in range(3)], axis=0
        )
        total = total + lax.dot_general(
            owner,
            parts,
            (((1,), (1,)), ((), ())),
            precision=EXACT,
            preferred_element_type=F32,
        )
    return total


def late_links_kernel(pull, lists, slots, dirs, out):
    pulls = [pull[i].reshape(576, 128) for i in range(2)]
    out[...] = link_gradient(pulls, lists, slots, dirs, (3, 2))


def start_kernel(
    right_msg,
    left_msg,
    from_left,
    from_right,
    pops,
    f1,
    n1,
    s1,
    n_own,
    s_own,
    late,
    lists,
    slots,
    dirs,
    a0_out,
    grad_out,
    a2,
    a1,
    pull,
):
    for q in range(19):
        for x in range(2):
            k = (q * 2 + x) * 2
            a2[q, x] = ext(from_left, k)
            a2[q, 2 + x] = ext(left_msg, k)
            a2[q, 4 + x] = ext(right_msg, k)
            a2[q, 6 + x] = ext(from_right, k)

    def first(i, carry):
        x = 1 + i
        out, rho, local = adjoint_at(
            lambda q: f1[q, i],
            lambda q, at: a2[q, at],
            x,
            lambda q: n1[q, i],
            lambda q: s1[q, i],
        )
        for q in range(19):
            a1[q, i] = out[q]

        @pl.when((i >= 1) & (i < 5))
        def _():
            for q in range(1, 19):
                pull[0, q - 1, i - 1] = ((-6.0 * WEIGHTS[q]) * rho * local[q])[:8]

        return carry

    lax.fori_loop(0, 6, first, 0)

    def last(i, carry):
        f = [pops[q, i] for q in range(19)]
        local = [a1[q, 1 + i] for q in range(19)]
        arrived = []
        for q in range(19):
            cx, cy, cz = VELOCITIES[q]
            value = a1[q, 1 + i + cx] if cx else local[q]
            arrived.append(shifted(value, -cy, -cz)[:8])
        local = [v[:8] for v in local]
        out, rho = adjoint_column(
            f, arrived, local, [n_own[q, i, 0:8] for q in range(18)], [s_own[q, i, 0:8] for q in range(18)]
        )
        for q in range(19):
            a0_out[q, i] = out[q]
        for q in range(1, 19):
            pull[1, q - 1, i] = (-6.0 * WEIGHTS[q]) * rho * local[q]
        return carry

    lax.fori_loop(0, 4, last, 0)
    pulls = [pull[i].reshape(576, 128) for i in range(2)]
    grad_out[...] = late[...] + link_gradient(pulls, lists, slots, dirs, (1, 0))


def ring(axis, step):
    count = lax.axis_size(axis)
    return [(i, (i + step) % count) for i in range(count)]


def shape(*dims, dtype=F32):
    return jax.ShapeDtypeStruct(dims, dtype)


def cost(flops, bytes_accessed):
    return pl.CostEstimate(flops=flops, bytes_accessed=bytes_accessed, transcendentals=0)


def shards(
    populations, wall_speed, adjoint_seed, link_cell, link_dir, link_node, live_links, node_slot
):
    vmem = full()
    smem = pl.BlockSpec(memory_space=pltpu.SMEM)
    hbm = pl.BlockSpec(memory_space=pl.ANY)
    copies = jnp.broadcast_to(wall_speed.reshape(1, 192), (32, 192))
    wall = lax.all_to_all(copies, "gy", split_axis=0, concat_axis=0, tiled=True)
    base = (lax.axis_index("gx") * 2048).astype(jnp.int32).reshape(1)
    up_msg, down_msg, lists, slots = pl.pallas_call(
        prep_kernel,
        name="prep",
        out_shape=[
            shape(Y_TILES, 8, 128),
            shape(Y_TILES, 8, 128),
            shape(8, 1024),
            shape(4, 1024, dtype=jnp.int32),
        ],
        in_specs=[smem] + [vmem] * 8,
        out_specs=[vmem] * 4,
    )(
        base,
        populations,
        adjoint_seed,
        wall,
        link_cell,
        link_dir,
        link_node,
        live_links,
        node_slot.reshape(128, 128),
    )
    from_down = lax.ppermute(up_msg, "gy", ring("gy", 1))
    from_up = lax.ppermute(down_msg, "gy", ring("gy", -1))
    right_msg, left_msg = pl.pallas_call(
        pack_kernel,
        name="pack",
        out_shape=[shape(X_TILES, 8, 128)] * 2,
        in_specs=[vmem] * 5,
        out_specs=[vmem] * 2,
    )(populations, adjoint_seed, from_up, from_down, lists)
    from_left = lax.ppermute(right_msg, "gx", ring("gx", 1))
    from_right = lax.ppermute(left_msg, "gx", ring("gx", -1))
    n_own, s_own = pl.pallas_call(
        own_links_kernel,
        name="own_links",
        out_shape=[shape(4, 18, 4, 16, 128)] * 2,
        in_specs=[vmem] * 3,
        out_specs=[vmem] * 2,
        cost_estimate=cost(5_000_000_000, 6_000_000),
        compiler_params=pltpu.CompilerParams(vmem_limit_bytes=48 << 20),
    )(lists, from_up, from_down)
    region = pltpu.VMEM((19, 12, 16, 128), F32)
    f1, n1, s1, a2, up_msg, down_msg, pull = pl.pallas_call(
        window_kernel,
        name="window",
        out_shape=[
            shape(19, 6, 16, 128),
            shape(18, 6, 16, 128),
            shape(18, 6, 16, 128),
            shape(19, 4, 8, 128),
            shape(19, 8, 128),
            shape(19, 8, 128),
            shape(2, 18, 4, 8, 128),
        ],
        in_specs=[vmem] * 4 + [hbm] * 2,
        out_specs=[vmem] * 7,
        scratch_shapes=[
            pltpu.VMEM((4, 18, 12, 16, 128), F32),
            pltpu.VMEM((4, 18, 12, 16, 128), F32),
            region,
            pltpu.VMEM((12, 16, 128), F32),
            region,
            region,
            region,
            region,
            pltpu.SemaphoreType.DMA((2,)),
        ],
        compiler_params=pltpu.CompilerParams(vmem_limit_bytes=58 << 20),
    )(right_msg, left_msg, from_left, from_right, n_own, s_own)
    from_down = lax.ppermute(up_msg, "gy", ring("gy", 1))
    from_up = lax.ppermute(down_msg, "gy", ring("gy", -1))
    right_msg, left_msg = pl.pallas_call(
        pack_adjoint_kernel,
        name="pack_adjoint",
        out_shape=[shape(SEED_TILES, 8, 128)] * 2,
        in_specs=[vmem] * 3,
        out_specs=[vmem] * 2,
    )(a2, from_up, from_down)
    from_left = lax.ppermute(right_msg, "gx", ring("gx", 1))
    from_right = lax.ppermute(left_msg, "gx", ring("gx", -1))
    late = pl.pallas_call(
        late_links_kernel,
        name="late_links",
        out_shape=shape(32, 192),
        in_specs=[vmem] * 4,
        out_specs=vmem,
        cost_estimate=cost(2_000_000_000, 2_000_000),
        compiler_params=pltpu.CompilerParams(vmem_limit_bytes=32 << 20),
    )(pull, lists, slots, link_dir)
    adjoint, owned = pl.pallas_call(
        start_kernel,
        name="start",
        out_shape=[shape(19, 4, 8, 128), shape(32, 192)],
        in_specs=[vmem] * 14,
        out_specs=[vmem] * 2,
        scratch_shapes=[
            pltpu.VMEM((19, 8, 16, 128), F32),
            pltpu.VMEM((19, 6, 16, 128), F32),
            pltpu.VMEM((2, 18, 4, 8, 128), F32),
        ],
        compiler_params=pltpu.CompilerParams(vmem_limit_bytes=48 << 20),
    )(
        right_msg,
        left_msg,
        from_left,
        from_right,
        populations,
        f1,
        n1,
        s1,
        n_own[0],
        s_own[0],
        late,
        lists,
        slots,
        link_dir,
    )
    arrived = lax.all_to_all(owned, "gy", split_axis=0, concat_axis=0, tiled=True)
    return (adjoint, arrived.sum(axis=0).reshape(3, 64))


def solution(mesh):
    placed = (
        P(None, "gx", "gy", None),
        P(None, ("gx", "gy")),
        P(None, "gx", "gy", None),
        P(None, ("gx", "gy")),
        P(None, ("gx", "gy")),
        P(None, ("gx", "gy")),
        P(None, ("gx", "gy")),
        P(),
    )
    return jax.shard_map(
        shards,
        mesh=mesh,
        in_specs=placed,
        out_specs=(P(None, "gx", "gy", None), P(None, ("gx", "gy"))),
        check_vma=False,
    )
```

```python
import jax
import jax.numpy as jnp
from jax import lax
from jax.experimental import pallas as pl
from jax.experimental.pallas import tpu as pltpu
from jax.sharding import PartitionSpec as P

VELOCITIES = [
    (0, 0, 0),
    (1, 0, 0),
    (-1, 0, 0),
    (0, 1, 0),
    (0, -1, 0),
    (0, 0, 1),
    (0, 0, -1),
    (1, 1, 0),
    (-1, -1, 0),
    (1, -1, 0),
    (-1, 1, 0),
    (1, 0, 1),
    (-1, 0, -1),
    (1, 0, -1),
    (-1, 0, 1),
    (0, 1, 1),
    (0, -1, -1),
    (0, 1, -1),
    (0, -1, 1),
]
WEIGHTS = [1.0 / 3.0] + [1.0 / 18.0] * 6 + [1.0 / 36.0] * 12
OPPOSITE = [0] + [q + 1 if q % 2 else q - 1 for q in range(1, 19)]
OMEGA = 1.6
F32 = jnp.float32
BF16 = jnp.bfloat16
EXACT = lax.Precision.HIGHEST

POP_TILES = 152
SEED_TILES = 76
LIST_TILES = 8
X_TILES = POP_TILES + SEED_TILES
Y_TILES = 38 + 19 + LIST_TILES
SIDE_COUNT = (3, 2, 1, 1)
SIDE_BASE = (0, 3, 5, 6)


def full(shape=None):
    return pl.BlockSpec(memory_space=pltpu.VMEM)


def row_iota(shape):
    return lax.broadcasted_iota(jnp.int32, shape, 0)


def signs(dirs, component):
    out = jnp.zeros(dirs.shape, F32)
    for q in range(1, 19):
        c = VELOCITIES[q][component]
        if c:
            out = jnp.where(dirs == q, float(c), out)
    return out


def low_half(shape):
    return lax.broadcasted_iota(jnp.int32, shape, len(shape) - 2) < 4


def front_kernel(
    base,
    live_hbm,
    pops_hbm,
    seed_hbm,
    wall_hbm,
    cell_hbm,
    dirs_hbm,
    node_hbm,
    table_hbm,
    up_msg,
    down_msg,
    lists,
    wall_copies,
    pops,
    seed,
    wall,
    cell,
    dirs,
    node,
    table,
    live,
    sems,
):
    pairs = (
        (wall_hbm, wall),
        (node_hbm, node),
        (table_hbm, table),
        (dirs_hbm, dirs),
        (cell_hbm, cell),
        (pops_hbm, pops),
        (seed_hbm, seed),
        (live_hbm, live),
    )
    copies = [pltpu.make_async_copy(a, b, sems.at[i]) for i, (a, b) in enumerate(pairs)]
    for copy in copies:
        copy.start()
    copies[0].wait()
    row = jnp.concatenate([wall[c : c + 1, :] for c in range(3)], axis=1)
    wall_copies[...] = jnp.broadcast_to(row.reshape(1, 1, 192), (32, 1, 192))
    for copy in copies[1:5] + copies[7:]:
        copy.wait()
    front_links(base, live, cell, dirs, node, table, up_msg, down_msg, lists)
    copies[5].wait()
    copies[6].wait()
    low = low_half((8, 128))
    pair = row_iota((8, 128)) // 2
    for q in range(19):
        for i in range(2):
            even = pops[q, 2 * i]
            odd = pltpu.roll(pops[q, 2 * i + 1], 4, 0)
            down_msg[2 * q + i] = jnp.where(low, even, odd)
            up_msg[2 * q + i] = jnp.where(low, odd, even)
        down_msg[38 + q], up_msg[38 + q] = edge_rows([seed[q, x] for x in range(4)], pair)


def front_links(base, live, cell, dirs, node, table, up_msg, down_msg, lists):
    slot_table = table[...]
    high = (slot_table // 128).astype(F32).astype(BF16)
    rest = (slot_table % 128).astype(F32).astype(BF16)
    both = jnp.concatenate([high, rest], axis=0)
    iota = iota256()
    lanes = row_iota((128, 1024))
    lane = lax.broadcasted_iota(jnp.int32, (1, 1024), 1)
    codes, owners = [], []
    for s in range(4):
        nodes = node[s : s + 1, :]
        hot = onehot((nodes % 128).astype(F32), 128, iota)
        picked = jnp.dot(both, hot, preferred_element_type=F32)
        match = lanes == nodes // 128
        slot_high = jnp.sum(jnp.where(match, picked[:128], 0.0), axis=0, keepdims=True)
        slot_rest = jnp.sum(jnp.where(match, picked[128:], 0.0), axis=0, keepdims=True)
        owners.append(slot_high * 128.0 + slot_rest - base[0].astype(F32))
        direction = dirs[s : s + 1, :]
        opposite = direction + 1 - 2 * ((direction + 1) % 2)
        code = opposite * 4096 + cell[s : s + 1, :]
        codes.append(jnp.where(lane < live[s], code, -1).astype(F32))
    table8 = jnp.concatenate(codes + owners, axis=0)
    lists[...] = table8
    for t in range(8):
        up_msg[57 + t] = table8[:, 128 * t : 128 * t + 128]
        down_msg[57 + t] = table8[:, 128 * t : 128 * t + 128]


def edge_rows(columns, pair):
    down = columns[0]
    up = pltpu.roll(columns[0], 2, 0)
    for x in range(1, 4):
        down = jnp.where(pair == x, pltpu.roll(columns[x], 2 * x, 0), down)
        up = jnp.where(pair == x, pltpu.roll(columns[x], 2 * x + 2, 0) if x < 3 else columns[x], up)
    return down, up


def push_kernel(wall, lists, from_up, from_down, out):
    owned = wall[...].reshape(32, 192)
    speeds = jnp.concatenate([owned[:, 64 * c : 64 * c + 64] for c in range(3)], axis=0)
    high = speeds.astype(BF16)
    rest = (speeds - high.astype(F32)).astype(BF16)
    last = (speeds - high.astype(F32) - rest.astype(F32)).astype(BF16)
    pieces = jnp.concatenate([high, rest, last], axis=0)
    iota = iota256()
    owner_iota = row_iota((32, 1024)).astype(F32)
    for k, table8 in enumerate((lists[...], read_list(from_up, 57), read_list(from_down, 57))):
        out[8 * k : 8 * k + 4, :] = table8[:4]
        for s in range(4):
            slot = table8[4 + s : 5 + s, :]
            owner = jnp.floor(slot * (1.0 / 64.0))
            place = slot - owner * 64.0
            picked = jnp.dot(pieces, onehot(place, 64, iota), preferred_element_type=F32)
            picked = picked[:96] + picked[96:192] + picked[192:]
            match = owner_iota == owner
            opposite = table8[s : s + 1, :].astype(jnp.int32) // 4096
            push = jnp.zeros((1, 1024), F32)
            for c in range(3):
                speed = jnp.sum(
                    jnp.where(match, picked[32 * c : 32 * c + 32], 0.0), axis=0, keepdims=True
                )
                push = push - signs(opposite, c) * speed
            out[8 * k + 4 + s : 8 * k + 5 + s, :] = push


def pack_kernel(pops, seed, from_up, from_down, right_msg, left_msg):
    low = low_half((8, 128))
    sub = row_iota((8, 128))
    for q in range(19):
        for i in range(2):
            up = from_up[2 * q + i]
            down = from_down[2 * q + i]
            even = jnp.where(low, up, down)
            odd = pltpu.roll(jnp.where(low, down, up), 4, 0)
            for x, halo in ((2 * i, even), (2 * i + 1, odd)):
                k = (q * 4 + x) * 2
                own = pops[q, x]
                for msg in (right_msg, left_msg):
                    msg[k] = own
                    msg[k + 1] = halo
        up = from_up[38 + q]
        down = from_down[38 + q]
        for x in range(4):
            halo = widen_two(up, down, x, sub)
            msg = left_msg if x < 2 else right_msg
            k = POP_TILES + (q * 2 + x % 2) * 2
            msg[k] = seed[q, x]
            msg[k + 1] = halo


def widen_two(up, down, x, sub):
    first = up if x == 0 else pltpu.roll(up, 8 - 2 * x, 0)
    last = down if x == 3 else pltpu.roll(down, 6 - 2 * x, 0)
    return jnp.where(sub < 4, first, last)


def onehot(code, rows, iota):
    out = []
    padded = (rows + 15) // 16 * 16
    for start in range(0, padded, 256):
        count = min(256, padded - start)
        wanted = jnp.clip(code - float(start), -1.0, 256.0).astype(BF16)
        out.append(
            jnp.concatenate(
                [
                    jnp.where(
                        iota[:count] == wanted[:, 128 * t : 128 * t + 128],
                        jnp.array(1.0, BF16),
                        jnp.array(0.0, BF16),
                    )
                    for t in range(8)
                ],
                axis=1,
            )
        )
    return out[0] if len(out) == 1 else jnp.concatenate(out, axis=0)


def iota256():
    return row_iota((256, 128)).astype(F32).astype(BF16)


def split_code(code):
    number = code.astype(jnp.int32)
    dead = number < 0
    z = jnp.where(dead, -1, number % 128)
    row = jnp.where(dead, 0, number // 128)
    return dead, row // 32 - 1, (row // 8) % 4, row % 8, z


def scatter_table(code, push, first, count, iota, part):
    dead, lane_q, x, y, z = split_code(code)
    index = lane_q * count + (x - first)
    outside = dead | (x < first) | (x >= first + count)
    if part == "all":
        row, rows = index * 8 + y, 144 * count
    elif part == "low":
        row, rows = index * 4 + y, 72 * count
        outside = outside | (y >= 4)
    else:
        row, rows = (index + 1 - 2 * (index % 2)) * 4 + y - 4, 72 * count
        outside = outside | (y < 4)
    target = onehot(jnp.where(outside, -1, row).astype(F32), rows, iota)
    zcode = z.astype(F32).astype(BF16)
    high = push.astype(BF16)
    mid = (push - high.astype(F32)).astype(BF16)
    last = (push - high.astype(F32) - mid.astype(F32)).astype(BF16)
    zero = jnp.array(0.0, BF16)
    blocks = [[], [], [], []]
    for t in range(8):
        cut = slice(128 * t, 128 * t + 128)
        match = iota[:128] == zcode[:, cut]
        blocks[0].append(jnp.where(match, jnp.array(1.0, BF16), zero))
        for b, piece in zip(blocks[1:], (high, mid, last)):
            b.append(jnp.where(match, piece[:, cut], zero))
    values = jnp.concatenate([jnp.concatenate(b, axis=1) for b in blocks], axis=0)
    dense = lax.dot_general(
        target, values, (((1,), (1,)), ((), ())), preferred_element_type=F32
    )[:rows]
    return dense[:, :128], dense[:, 128:256] + dense[:, 256:384] + dense[:, 384:]


def scatter_columns(lists, s, index, first, count, iota, n_ref, s_ref, where):
    own, up, down = lists
    n, p = scatter_table(own[s : s + 1, :], own[4 + s : 5 + s, :], first, count, iota, "all")
    at = pl.ds(where, count)
    n_ref[index, :, at, 0:8, :] = n.reshape(18, count, 8, 128)
    s_ref[index, :, at, 0:8, :] = p.reshape(18, count, 8, 128)
    above = scatter_table(up[s : s + 1, :], up[4 + s : 5 + s, :], first, count, iota, "low")
    below = scatter_table(down[s : s + 1, :], down[4 + s : 5 + s, :], first, count, iota, "high")
    shape = (9 * count, 8, 128)
    low = low_half(shape)
    for ref, a, b in zip((n_ref, s_ref), above, below):
        a, b = a.reshape(shape), b.reshape(shape)
        even = jnp.where(low, a, b)
        odd = pltpu.roll(jnp.where(low, b, a), 4, 1)
        halo = jnp.stack([even, odd], axis=1).reshape(18, count, 8, 128)
        ref[index, :, at, 8:16, :] = halo


def read_list(ref, start):
    return jnp.concatenate([ref[start + t] for t in range(8)], axis=1)


def own_links_kernel(lists, n_ref, s_ref):
    iota = iota256()
    three = [lists[8 * k : 8 * k + 8, :] for k in range(3)]
    for s in range(4):
        scatter_columns(three, s, s, 0, 4, iota, n_ref, s_ref, 0)


def side_links_kernel(from_left, from_right, n_ref, s_ref):
    iota = iota256()
    for side, ref in enumerate((from_left, from_right)):
        three = [ref[8 * k : 8 * k + 8, :] for k in range(3)]
        for s in range(4):
            count = SIDE_COUNT[s]
            first = 0 if side else 4 - count
            scatter_columns(three, s, side, first, count, iota, n_ref, s_ref, SIDE_BASE[s])


def column_groups(s, n_own, s_own, n_side, s_side):
    count, base = SIDE_COUNT[s], SIDE_BASE[s]
    return (
        (4 - count, count, lambda q, i: n_side[0, q, base + i], lambda q, i: s_side[0, q, base + i]),
        (4, 4, lambda q, i: n_own[s, q, i], lambda q, i: s_own[s, q, i]),
        (8, count, lambda q, i: n_side[1, q, base + i], lambda q, i: s_side[1, q, base + i]),
    )


def shifted(value, cy, cz):
    if cy:
        value = pltpu.roll(value, cy % 16, 0)
    if cz:
        value = pltpu.roll(value, cz % 128, 1)
    return value


def moments(f):
    rho = f[0]
    for q in range(1, 19):
        rho = rho + f[q]
    inverse = 1.0 / rho
    speeds = []
    for c in range(3):
        total = None
        for q in range(1, 19):
            v = VELOCITIES[q][c]
            if v:
                total = (f[q] if v > 0 else -f[q]) if total is None else (total + f[q] if v > 0 else total - f[q])
        speeds.append(total * inverse)
    return rho, speeds


def along(speeds, q):
    total = None
    for c in range(3):
        v = VELOCITIES[q][c]
        if v:
            term = speeds[c] if v > 0 else -speeds[c]
            total = term if total is None else total + term
    return total


def collide_column(f):
    rho, speeds = moments(f)
    rest = 1.0 - 1.5 * (speeds[0] * speeds[0] + speeds[1] * speeds[1] + speeds[2] * speeds[2])
    out = [(1.0 - OMEGA) * f[0] + (OMEGA * WEIGHTS[0]) * rho * rest]
    for q in range(1, 19, 2):
        cu = along(speeds, q)
        scale = (OMEGA * WEIGHTS[q]) * rho
        even = scale * (rest + 4.5 * cu * cu)
        odd = scale * (3.0 * cu)
        out.append((1.0 - OMEGA) * f[q] + (even + odd))
        out.append((1.0 - OMEGA) * f[q + 1] + (even - odd))
    return out, rho


def collide_into(load, start, count, relaxed, density):
    def body(i, carry):
        f = [load(q, i) for q in range(19)]
        g, rho = collide_column(f)
        for q in range(19):
            relaxed[q, start + i] = g[q]
        density[start + i] = rho
        return carry

    lax.fori_loop(0, count, body, 0)


def stream_into(relaxed, density, groups, out):
    for start, count, counts, pushes in groups:

        def body(i, carry):
            x = start + i
            rho = density[x]
            out[0, x] = relaxed[0, x]
            for q in range(1, 19):
                p = OPPOSITE[q]
                cx, cy, cz = VELOCITIES[q]
                moved = shifted(relaxed[q, x - cx], cy, cz)
                bounce = (0.5 * counts(q - 1, i)) * (relaxed[p, x] - relaxed[q, x])
                push = (6.0 * WEIGHTS[q]) * rho * pushes(q - 1, i)
                out[q, x] = moved + (bounce - push)
            return carry

        lax.fori_loop(0, count, body, 0)


def adjoint_column(f, arrived, local, counts, pushes):
    rho, speeds = moments(f)
    b = [arrived[0]]
    direct = None
    for q in range(1, 19):
        p = OPPOSITE[q]
        b.append(
            arrived[q] + 0.5 * (counts[p - 1] * local[p] - counts[q - 1] * local[q])
        )
        term = (6.0 * WEIGHTS[q]) * (pushes[q - 1] * local[q])
        direct = term if direct is None else direct + term
    beta = [WEIGHTS[q] * b[q] for q in range(19)]
    total = beta[0]
    first = [None] * 3
    second = [None] * 3
    for q in range(1, 19, 2):
        plus = beta[q] + beta[q + 1]
        minus = beta[q] - beta[q + 1]
        total = total + plus
        inner = along(speeds, q) * plus
        for c in range(3):
            v = VELOCITIES[q][c]
            if v:
                m = minus if v > 0 else -minus
                k = inner if v > 0 else -inner
                first[c] = m if first[c] is None else first[c] + m
                second[c] = k if second[c] is None else second[c] + k
    square = speeds[0] * speeds[0] + speeds[1] * speeds[1] + speeds[2] * speeds[2]
    curved = speeds[0] * second[0] + speeds[1] * second[1] + speeds[2] * second[2]
    rest = OMEGA * (total - 4.5 * curved + 1.5 * square * total) - direct
    slopes = [
        OMEGA * (3.0 * first[c] + 9.0 * second[c] - 3.0 * speeds[c] * total) for c in range(3)
    ]
    out = [(1.0 - OMEGA) * b[0] + rest]
    for q in range(1, 19, 2):
        cu = along(slopes, q)
        out.append((1.0 - OMEGA) * b[q] + (rest + cu))
        out.append((1.0 - OMEGA) * b[q + 1] + (rest - cu))
    return out, rho


def adjoint_at(load_f, adjoint, x, counts, pushes):
    f = [load_f(q) for q in range(19)]
    local = [adjoint(q, x) for q in range(19)]
    arrived = []
    for q in range(19):
        cx, cy, cz = VELOCITIES[q]
        value = adjoint(q, x + cx) if cx else local[q]
        arrived.append(shifted(value, -cy, -cz))
    out, rho = adjoint_column(
        f, arrived, local, [counts(q) for q in range(18)], [pushes(q) for q in range(18)]
    )
    return out, rho, local


def ext(ref, k):
    return jnp.concatenate([ref[k], ref[k + 1]], axis=0)


def window_kernel(
    right_msg,
    left_msg,
    from_left,
    from_right,
    n_own,
    s_own,
    n_side,
    s_side,
    f1_out,
    a2_out,
    up_msg,
    down_msg,
    pull,
    relaxed,
    density,
    f2,
    f3,
    a4,
    a3,
):
    def groups(s):
        return column_groups(s, n_own, s_own, n_side, s_side)

    for ref, start in ((from_left, 0), (right_msg, 4), (from_right, 8)):

        def load(q, i, ref=ref):
            return ref[pl.ds((q * 4 + i) * 2, 2)].reshape(16, 128)

        collide_into(load, start, 4, relaxed, density)
    stream_into(relaxed, density, groups(0), f2)
    for q in range(19):
        f1_out[q] = f2[q, 3:9]
    collide_into(lambda q, i: f2[q, 1 + i], 1, 10, relaxed, density)
    stream_into(relaxed, density, groups(1), f2)
    collide_into(lambda q, i: f2[q, 2 + i], 2, 8, relaxed, density)
    stream_into(relaxed, density, groups(2), f3)
    for q in range(19):
        for x in range(2):
            k = POP_TILES + (q * 2 + x) * 2
            a4[q, 2 + x] = ext(from_left, k)
            a4[q, 4 + x] = ext(left_msg, k)
            a4[q, 6 + x] = ext(right_msg, k)
            a4[q, 8 + x] = ext(from_right, k)
    for start, count, counts, pushes in groups(3):

        def third(i, carry, start=start, count=count, counts=counts, pushes=pushes):
            x = start + i
            out, rho, local = adjoint_at(
                lambda q: f3[q, x],
                lambda q, at: a4[q, at],
                x,
                lambda q: counts(q, i),
                lambda q: pushes(q, i),
            )
            for q in range(19):
                a3[q, x] = out[q]
            if count == 4:
                for q in range(1, 19):
                    pull[0, q - 1, i] = ((-6.0 * WEIGHTS[q]) * rho * local[q])[:8]
            return carry

        lax.fori_loop(0, count, third, 0)

    def second(i, carry):
        x = 4 + i
        out, rho, local = adjoint_at(
            lambda q: f2[q, x],
            lambda q, at: a3[q, at],
            x,
            lambda q: n_own[2, q, i],
            lambda q: s_own[2, q, i],
        )
        rho1 = f1_out[0, 1 + i]
        for q in range(1, 19):
            rho1 = rho1 + f1_out[q, 1 + i]
        for q in range(19):
            a2_out[q, i] = out[q][:8]
        for q in range(1, 19):
            pull[1, q - 1, i] = ((-6.0 * WEIGHTS[q]) * rho * local[q])[:8]
            pull[2, q - 1, i] = ((-6.0 * WEIGHTS[q]) * rho1 * out[q])[:8]
        return carry

    lax.fori_loop(0, 4, second, 0)
    pair = row_iota((8, 128)) // 2
    for q in range(19):
        down_msg[q], up_msg[q] = edge_rows([a2_out[q, x] for x in range(4)], pair)


OUTWARD = tuple(tuple(q for q in range(19) if VELOCITIES[q][0] == c) for c in (-1, 1))
A_TILES = 48


def pack_adjoint_kernel(a2, from_up, from_down, right_msg, left_msg, middle):
    sub = row_iota((8, 128))
    for q in range(19):
        for x in range(4):
            own, halo = a2[q, x], widen_two(from_up[q], from_down[q], x, sub)
            if x in (0, 3):
                msg, k = (left_msg if x == 0 else right_msg), 2 * q
            else:
                msg, k = middle, (q * 2 + x - 1) * 2
            msg[k] = own
            msg[k + 1] = halo
            for side, edge in ((right_msg, 0), (left_msg, 1)):
                if x == 2 - edge and q in OUTWARD[edge]:
                    k = 38 + 2 * OUTWARD[edge].index(q)
                    side[k] = own
                    side[k + 1] = halo


def link_gradient(pulls, lists, steps):
    iota = iota256()
    total = jnp.zeros((32, 192), F32)
    lanes = row_iota((128, 1024))
    for i, s in enumerate(steps):
        code = lists[s : s + 1, :]
        dead, lane_q, x, y, z = split_code(code)
        row = jnp.where(dead, -1, lane_q * 32 + x * 8 + y).astype(F32)
        hot = onehot(row, 576, iota)
        high = pulls[i].astype(BF16)
        rest = (pulls[i] - high.astype(F32)).astype(BF16)
        low = (pulls[i] - high.astype(F32) - rest.astype(F32)).astype(BF16)
        picked = lax.dot_general(
            jnp.concatenate([high, rest, low], axis=1),
            hot,
            (((0,), (0,)), ((), ())),
            preferred_element_type=F32,
        )
        match = lanes == z
        value = jnp.sum(
            jnp.where(match, picked[:128] + picked[128:256] + picked[256:], 0.0),
            axis=0,
            keepdims=True,
        )
        slot = lists[4 + s : 5 + s, :].astype(jnp.int32)
        opposite = code.astype(jnp.int32) // 4096
        owner = jnp.where(row_iota((32, 1024)) == slot // 64, 1.0, 0.0)
        place = row_iota((64, 1024)) == slot % 64
        parts = jnp.concatenate(
            [jnp.where(place, -value * signs(opposite, c), 0.0) for c in range(3)], axis=0
        )
        total = total + lax.dot_general(
            owner,
            parts,
            (((1,), (1,)), ((), ())),
            precision=EXACT,
            preferred_element_type=F32,
        )
    return total


def late_links_kernel(pull, lists, out):
    pulls = [pull[i].reshape(576, 128) for i in range(2)]
    out[...] = link_gradient(pulls, lists, (3, 2))


def early_links_kernel(pull, lists, late, out):
    out[...] = late[...] + link_gradient([pull[2].reshape(576, 128)], lists, (1,))


def first_adjoint_kernel(
    right_msg,
    left_msg,
    middle,
    from_left,
    from_right,
    pops,
    f1,
    n_own,
    s_own,
    n_side,
    s_side,
    late,
    lists,
    a1,
    grad_out,
    a2,
    pull,
):
    for q in range(19):
        a2[q, 1] = ext(from_left, 2 * q)
        a2[q, 2] = ext(left_msg, 2 * q)
        a2[q, 3] = ext(middle, 4 * q)
        a2[q, 4] = ext(middle, 4 * q + 2)
        a2[q, 5] = ext(right_msg, 2 * q)
        a2[q, 6] = ext(from_right, 2 * q)
    for i in range(5):
        a2[OUTWARD[0][i], 0] = ext(from_left, 38 + 2 * i)
        a2[OUTWARD[1][i], 7] = ext(from_right, 38 + 2 * i)
    left, own, right = column_groups(1, n_own, s_own, n_side, s_side)
    for at, count, group, skip in ((0, 1, left, 1), (1, 4, own, 0), (5, 1, right, 0)):

        def first(i, carry, at=at, count=count, group=group, skip=skip):
            out, rho, local = adjoint_at(
                lambda q: f1[q, at + i],
                lambda q, x: a2[q, x],
                at + i + 1,
                lambda q: group[2](q, i + skip),
                lambda q: group[3](q, i + skip),
            )
            for q in range(19):
                a1[q, at + i] = out[q]
            if count == 4:
                rho0 = pops[0, i]
                for q in range(1, 19):
                    rho0 = rho0 + pops[q, i]
                for q in range(1, 19):
                    pull[q - 1, i] = (-6.0 * WEIGHTS[q]) * rho0 * out[q][:8]
            return carry

        lax.fori_loop(0, count, first, 0)
    total = late[...] + link_gradient([pull[...].reshape(576, 128)], lists, (0,))
    grad_out[...] = total.reshape(32, 1, 192)


def total_kernel(parts, out):
    total = parts[0]
    for k in range(1, 32):
        total = total + parts[k]
    for c in range(3):
        out[c : c + 1, :] = total[:, 64 * c : 64 * c + 64]


def last_adjoint_kernel(a1, pops, n_own, s_own, a0_out):
    def last(i, carry):
        f = [pops[q, i] for q in range(19)]
        local = [a1[q, 1 + i] for q in range(19)]
        arrived = []
        for q in range(19):
            cx, cy, cz = VELOCITIES[q]
            value = a1[q, 1 + i + cx] if cx else local[q]
            arrived.append(shifted(value, -cy, -cz)[:8])
        local = [v[:8] for v in local]
        out, _ = adjoint_column(
            f,
            arrived,
            local,
            [n_own[0, q, i, 0:8] for q in range(18)],
            [s_own[0, q, i, 0:8] for q in range(18)],
        )
        for q in range(19):
            a0_out[q, i] = out[q]
        return carry

    lax.fori_loop(0, 4, last, 0)


def ring(axis, step):
    count = lax.axis_size(axis)
    return [(i, (i + step) % count) for i in range(count)]


def shape(*dims, dtype=F32):
    return jax.ShapeDtypeStruct(dims, dtype)


def cost(flops, bytes_accessed):
    return pl.CostEstimate(flops=flops, bytes_accessed=bytes_accessed, transcendentals=0)


def call(kernel, name, out_shape, count, limit, scratch=(), smem=0, flops=0, moved=0):
    vmem = full()
    many = isinstance(out_shape, list)
    return pl.pallas_call(
        kernel,
        name=name,
        out_shape=out_shape,
        in_specs=[pl.BlockSpec(memory_space=pltpu.SMEM)] * smem + [vmem] * (count - smem),
        out_specs=[vmem] * len(out_shape) if many else vmem,
        scratch_shapes=list(scratch),
        cost_estimate=cost(flops, moved) if flops else None,
        compiler_params=pltpu.CompilerParams(vmem_limit_bytes=limit << 20),
    )


def shards(
    populations, wall_speed, adjoint_seed, link_cell, link_dir, link_node, live_links, node_slot
):
    base = (lax.axis_index("gx") * 2048).astype(jnp.int32).reshape(1)
    smem = pl.BlockSpec(memory_space=pltpu.SMEM)
    operands = (
        populations,
        adjoint_seed,
        wall_speed,
        link_cell,
        link_dir,
        link_node,
        node_slot.reshape(128, 128),
    )
    up_msg, down_msg, lists, copies = pl.pallas_call(
        front_kernel,
        name="front",
        out_shape=[
            shape(Y_TILES, 8, 128),
            shape(Y_TILES, 8, 128),
            shape(8, 1024),
            shape(32, 1, 192),
        ],
        in_specs=[smem] + [pl.BlockSpec(memory_space=pltpu.HBM)] * 8,
        out_specs=[full()] * 4,
        scratch_shapes=[pltpu.VMEM(a.shape, a.dtype) for a in operands]
        + [pltpu.SMEM((4,), jnp.int32), pltpu.SemaphoreType.DMA((8,))],
        compiler_params=pltpu.CompilerParams(vmem_limit_bytes=12 << 20),
    )(
        base,
        *(
            pltpu.with_memory_space_constraint(a, pltpu.HBM)
            for a in (live_links.reshape(4), *operands)
        ),
    )
    from_down = lax.ppermute(up_msg, "gy", ring("gy", 1))
    from_up = lax.ppermute(down_msg, "gy", ring("gy", -1))
    wall = lax.all_to_all(copies, "gy", split_axis=0, concat_axis=0, tiled=True)
    all_lists = call(push_kernel, "push", shape(24, 1024), 4, 8, flops=500_000_000, moved=500_000)(
        wall, lists, from_up, from_down
    )
    left_lists = lax.ppermute(all_lists, "gx", ring("gx", 1))
    right_lists = lax.ppermute(all_lists, "gx", ring("gx", -1))
    right_msg, left_msg = call(pack_kernel, "pack", [shape(X_TILES, 8, 128)] * 2, 4, 8)(
        populations, adjoint_seed, from_up, from_down
    )
    from_left = lax.ppermute(right_msg, "gx", ring("gx", 1))
    from_right = lax.ppermute(left_msg, "gx", ring("gx", -1))
    n_own, s_own = call(
        own_links_kernel,
        "own_links",
        [shape(4, 18, 4, 16, 128)] * 2,
        1,
        24,
        flops=5_000_000_000,
        moved=5_000_000,
    )(all_lists)
    n_side, s_side = call(
        side_links_kernel,
        "side_links",
        [shape(2, 18, 7, 16, 128)] * 2,
        2,
        24,
        flops=5_000_000_000,
        moved=5_000_000,
    )(left_lists, right_lists)
    region = pltpu.VMEM((19, 12, 16, 128), F32)
    f1, a2, up_msg, down_msg, pull = call(
        window_kernel,
        "window",
        [
            shape(19, 6, 16, 128),
            shape(19, 4, 8, 128),
            shape(19, 8, 128),
            shape(19, 8, 128),
            shape(3, 18, 4, 8, 128),
        ],
        8,
        30,
        [region, pltpu.VMEM((12, 16, 128), F32), region, region, region, region],
    )(right_msg, left_msg, from_left, from_right, n_own, s_own, n_side, s_side)
    from_down = lax.ppermute(up_msg, "gy", ring("gy", 1))
    from_up = lax.ppermute(down_msg, "gy", ring("gy", -1))
    late = call(
        late_links_kernel, "late_links", shape(32, 192), 2, 16, flops=2_000_000_000, moved=2_000_000
    )(pull, lists)
    late, from_up, from_down = lax.optimization_barrier((late, from_up, from_down))
    right_msg, left_msg, middle = call(
        pack_adjoint_kernel,
        "pack_adjoint",
        [shape(A_TILES, 8, 128), shape(A_TILES, 8, 128), shape(SEED_TILES, 8, 128)],
        3,
        4,
    )(a2, from_up, from_down)
    from_left = lax.ppermute(right_msg, "gx", ring("gx", 1))
    from_right = lax.ppermute(left_msg, "gx", ring("gx", -1))
    late = call(
        early_links_kernel,
        "early_links",
        shape(32, 192),
        3,
        16,
        flops=1_000_000_000,
        moved=1_000_000,
    )(pull, lists, late)
    a1, owned = call(
        first_adjoint_kernel,
        "first_adjoint",
        [shape(19, 6, 16, 128), shape(32, 1, 192)],
        13,
        24,
        [pltpu.VMEM((19, 8, 16, 128), F32), pltpu.VMEM((18, 4, 8, 128), F32)],
    )(
        right_msg,
        left_msg,
        middle,
        from_left,
        from_right,
        populations,
        f1,
        n_own,
        s_own,
        n_side,
        s_side,
        late,
        lists,
    )
    arrived = lax.all_to_all(owned, "gy", split_axis=0, concat_axis=0, tiled=True)
    adjoint = call(
        last_adjoint_kernel,
        "last_adjoint",
        shape(19, 4, 8, 128),
        4,
        12,
        flops=10_000_000,
        moved=4_000_000,
    )(a1, populations, n_own, s_own)
    gradient = call(total_kernel, "total", shape(3, 64), 1, 4)(arrived)
    return (adjoint, gradient)


def solution(mesh):
    placed = (
        P(None, "gx", "gy", None),
        P(None, ("gx", "gy")),
        P(None, "gx", "gy", None),
        P(None, ("gx", "gy")),
        P(None, ("gx", "gy")),
        P(None, ("gx", "gy")),
        P(None, ("gx", "gy")),
        P(),
    )
    return jax.shard_map(
        shards,
        mesh=mesh,
        in_specs=placed,
        out_specs=(P(None, "gx", "gy", None), P(None, ("gx", "gy"))),
        check_vma=False,
    )
```

```python
import jax
import jax.numpy as jnp
from jax import lax
from jax.experimental import pallas as pl
from jax.experimental.pallas import tpu as pltpu
from jax.sharding import PartitionSpec as P

VELOCITIES = [
    (0, 0, 0),
    (1, 0, 0),
    (-1, 0, 0),
    (0, 1, 0),
    (0, -1, 0),
    (0, 0, 1),
    (0, 0, -1),
    (1, 1, 0),
    (-1, -1, 0),
    (1, -1, 0),
    (-1, 1, 0),
    (1, 0, 1),
    (-1, 0, -1),
    (1, 0, -1),
    (-1, 0, 1),
    (0, 1, 1),
    (0, -1, -1),
    (0, 1, -1),
    (0, -1, 1),
]
WEIGHTS = [1.0 / 3.0] + [1.0 / 18.0] * 6 + [1.0 / 36.0] * 12
OPPOSITE = [0] + [q + 1 if q % 2 else q - 1 for q in range(1, 19)]
OMEGA = 1.6
F32 = jnp.float32
BF16 = jnp.bfloat16
F8 = jnp.float8_e4m3fn
EXACT = lax.Precision.HIGHEST

POP_TILES = 152
SEED_TILES = 76
LIST_TILES = 8
FAR_POPS, NEAR_SEED, FAR_SEED, X_TILES = 114, 124, 162, 172
OUTWARD = tuple(tuple(q for q in range(19) if VELOCITIES[q][0] == c) for c in (-1, 1))
Y_TILES = 38 + 19 + LIST_TILES
SIDE_COUNT = (3, 2, 1, 1)
SIDE_BASE = (0, 3, 5, 6)


def full(shape=None):
    return pl.BlockSpec(memory_space=pltpu.VMEM)


def row_iota(shape):
    return lax.broadcasted_iota(jnp.int32, shape, 0)


def signs(dirs, component):
    out = jnp.zeros(dirs.shape, F32)
    for q in range(1, 19):
        c = VELOCITIES[q][component]
        if c:
            out = jnp.where(dirs == q, float(c), out)
    return out


def low_half(shape):
    return lax.broadcasted_iota(jnp.int32, shape, len(shape) - 2) < 4


def front_kernel(
    base,
    live_hbm,
    pops_hbm,
    seed_hbm,
    wall_hbm,
    cell_hbm,
    dirs_hbm,
    node_hbm,
    table_hbm,
    up_msg,
    down_msg,
    lists,
    wall_copies,
    pops,
    seed,
    wall,
    cell,
    dirs,
    node,
    table,
    live,
    sems,
):
    pairs = (
        (wall_hbm, wall),
        (node_hbm, node),
        (table_hbm, table),
        (dirs_hbm, dirs),
        (cell_hbm, cell),
        (pops_hbm, pops),
        (seed_hbm, seed),
        (live_hbm, live),
    )
    copies = [pltpu.make_async_copy(a, b, sems.at[i]) for i, (a, b) in enumerate(pairs)]
    for copy in copies:
        copy.start()
    copies[0].wait()
    row = jnp.concatenate([wall[c : c + 1, :] for c in range(3)], axis=1)
    wall_copies[...] = jnp.broadcast_to(row.reshape(1, 1, 192), (32, 1, 192))
    for copy in copies[1:5] + copies[7:]:
        copy.wait()
    front_links(base, live, cell, dirs, node, table, up_msg, down_msg, lists)
    copies[5].wait()
    copies[6].wait()
    low = low_half((8, 128))
    pair = row_iota((8, 128)) // 2
    for q in range(19):
        for i in range(2):
            even = pops[q, 2 * i]
            odd = pltpu.roll(pops[q, 2 * i + 1], 4, 0)
            down_msg[2 * q + i] = jnp.where(low, even, odd)
            up_msg[2 * q + i] = jnp.where(low, odd, even)
        down_msg[38 + q], up_msg[38 + q] = edge_rows([seed[q, x] for x in range(4)], pair)


def front_links(base, live, cell, dirs, node, table, up_msg, down_msg, lists):
    slot_table = table[...]
    high = (slot_table // 128).astype(F32).astype(BF16)
    rest = (slot_table % 128).astype(F32).astype(BF16)
    both = jnp.concatenate([high, rest], axis=0)
    iota = iota256()
    lanes = row_iota((128, 1024))
    lane = lax.broadcasted_iota(jnp.int32, (1, 1024), 1)
    codes, owners = [], []
    for s in range(4):
        nodes = node[s : s + 1, :]
        hot = onehot((nodes % 128).astype(F32), 128, iota)
        picked = jnp.dot(both, hot, preferred_element_type=F32)
        match = lanes == nodes // 128
        slot_high = jnp.sum(jnp.where(match, picked[:128], 0.0), axis=0, keepdims=True)
        slot_rest = jnp.sum(jnp.where(match, picked[128:], 0.0), axis=0, keepdims=True)
        owners.append(slot_high * 128.0 + slot_rest - base[0].astype(F32))
        direction = dirs[s : s + 1, :]
        opposite = direction + 1 - 2 * ((direction + 1) % 2)
        code = opposite * 4096 + cell[s : s + 1, :]
        codes.append(jnp.where(lane < live[s], code, -1).astype(F32))
    table8 = jnp.concatenate(codes + owners, axis=0)
    lists[...] = table8
    for t in range(8):
        up_msg[57 + t] = table8[:, 128 * t : 128 * t + 128]
        down_msg[57 + t] = table8[:, 128 * t : 128 * t + 128]


def edge_rows(columns, pair):
    down = columns[0]
    up = pltpu.roll(columns[0], 2, 0)
    for x in range(1, 4):
        down = jnp.where(pair == x, pltpu.roll(columns[x], 2 * x, 0), down)
        up = jnp.where(pair == x, pltpu.roll(columns[x], 2 * x + 2, 0) if x < 3 else columns[x], up)
    return down, up


def push_kernel(wall, lists, from_up, from_down, out):
    owned = wall[...].reshape(32, 192)
    speeds = jnp.concatenate([owned[:, 64 * c : 64 * c + 64] for c in range(3)], axis=0)
    high = speeds.astype(BF16)
    rest = (speeds - high.astype(F32)).astype(BF16)
    pieces = jnp.concatenate([high, rest], axis=0)
    iota = iota256()
    owner_iota = row_iota((32, 1024)).astype(F32)
    for k, table8 in enumerate((lists[...], read_list(from_up, 57), read_list(from_down, 57))):
        out[8 * k : 8 * k + 4, :] = table8[:4]
        for s in range(4):
            slot = table8[4 + s : 5 + s, :]
            owner = jnp.floor(slot * (1.0 / 64.0))
            place = slot - owner * 64.0
            picked = jnp.dot(pieces, onehot(place, 64, iota), preferred_element_type=F32)
            picked = picked[:96] + picked[96:]
            match = owner_iota == owner
            opposite = table8[s : s + 1, :].astype(jnp.int32) // 4096
            push = jnp.zeros((1, 1024), F32)
            for c in range(3):
                speed = jnp.sum(
                    jnp.where(match, picked[32 * c : 32 * c + 32], 0.0), axis=0, keepdims=True
                )
                push = push - signs(opposite, c) * speed
            out[8 * k + 4 + s : 8 * k + 5 + s, :] = push


def extended(pops, seed, from_up, from_down, low, sub):
    for q in range(19):
        for i in range(2):
            up = from_up[2 * q + i]
            down = from_down[2 * q + i]
            yield 0, q, 2 * i, pops[q, 2 * i], jnp.where(low, up, down)
            odd = pltpu.roll(jnp.where(low, down, up), 4, 0)
            yield 0, q, 2 * i + 1, pops[q, 2 * i + 1], odd
        for x in range(4):
            yield 1, q, x, seed[q, x], widen_two(from_up[38 + q], from_down[38 + q], x, sub)


def pack_kernel(pops, seed, from_up, from_down, right_msg, left_msg, edge):
    low = low_half((8, 128))
    sub = row_iota((8, 128))
    for kind, q, x, own, halo in extended(pops, seed, from_up, from_down, low, sub):
        places = []
        if kind == 0:
            if x >= 1:
                places.append((right_msg, (q * 3 + x - 1) * 2))
            if x <= 2:
                places.append((left_msg, (q * 3 + x) * 2))
            if x in (0, 3):
                places.append((edge, (q * 2 + x // 3) * 2))
        elif x in (0, 3):
            places.append((left_msg if x == 0 else right_msg, NEAR_SEED + 2 * q))
        elif q in OUTWARD[2 - x]:
            side = left_msg if x == 1 else right_msg
            places.append((side, FAR_SEED + 2 * OUTWARD[2 - x].index(q)))
        for msg, k in places:
            msg[k] = own
            msg[k + 1] = halo
    for msg, x, moving in ((right_msg, 0, OUTWARD[1]), (left_msg, 1, OUTWARD[0])):
        g, _ = collide_column([ext(edge, (q * 2 + x) * 2) for q in range(19)])
        for i, q in enumerate(moving):
            msg[FAR_POPS + 2 * i] = g[q][:8]
            msg[FAR_POPS + 2 * i + 1] = g[q][8:]


def widen_two(up, down, x, sub):
    first = up if x == 0 else pltpu.roll(up, 8 - 2 * x, 0)
    last = down if x == 3 else pltpu.roll(down, 6 - 2 * x, 0)
    return jnp.where(sub < 4, first, last)


def onehot(code, rows, iota):
    out = []
    padded = (rows + 15) // 16 * 16
    for start in range(0, padded, 256):
        count = min(256, padded - start)
        wanted = jnp.clip(code - float(start), -1.0, 256.0).astype(BF16)
        out.append(
            jnp.concatenate(
                [
                    jnp.where(
                        iota[:count] == wanted[:, 128 * t : 128 * t + 128],
                        jnp.array(1.0, BF16),
                        jnp.array(0.0, BF16),
                    )
                    for t in range(8)
                ],
                axis=1,
            )
        )
    return out[0] if len(out) == 1 else jnp.concatenate(out, axis=0)


def iota256():
    return row_iota((256, 128)).astype(F32).astype(BF16)


def split_code(code):
    number = code.astype(jnp.int32)
    dead = number < 0
    z = jnp.where(dead, -1, number % 128)
    row = jnp.where(dead, 0, number // 128)
    return dead, row // 32 - 1, (row // 8) % 4, row % 8, z


def scatter_table(code, push, first, count, iota, part):
    dead, lane_q, x, y, z = split_code(code)
    index = lane_q * count + (x - first)
    outside = dead | (x < first) | (x >= first + count)
    if part == "all":
        row, rows = index * 8 + y, 144 * count
    elif part == "low":
        row, rows = index * 4 + y, 72 * count
        outside = outside | (y >= 4)
    else:
        row, rows = (index + 1 - 2 * (index % 2)) * 4 + y - 4, 72 * count
        outside = outside | (y < 4)
    target = onehot(jnp.where(outside, -1, row).astype(F32), rows, iota)
    zcode = z.astype(F32).astype(BF16)
    scaled = push * 256.0
    high = scaled.astype(F8).astype(BF16)
    scaled = (scaled - high.astype(F32)) * 16.0
    mid = scaled.astype(F8).astype(BF16)
    scaled = (scaled - mid.astype(F32)) * 16.0
    last = scaled.astype(F8).astype(BF16)
    zero = jnp.array(0.0, BF16)
    blocks = [[], [], [], []]
    for t in range(8):
        cut = slice(128 * t, 128 * t + 128)
        match = iota[:128] == zcode[:, cut]
        blocks[0].append(jnp.where(match, jnp.array(1.0, BF16), zero))
        for b, piece in zip(blocks[1:], (high, mid, last)):
            b.append(jnp.where(match, piece[:, cut], zero))
    values = jnp.concatenate([jnp.concatenate(b, axis=1) for b in blocks], axis=0)
    dense = lax.dot_general(
        target.astype(F8), values.astype(F8), (((1,), (1,)), ((), ())), preferred_element_type=F32
    )[:rows]
    total = (
        dense[:, 128:256] * (1.0 / 256.0)
        + dense[:, 256:384] * (1.0 / 4096.0)
        + dense[:, 384:] * (1.0 / 65536.0)
    )
    return dense[:, :128], total


def scatter_columns(lists, s, index, first, count, iota, n_ref, s_ref, where):
    own, up, down = lists
    n, p = scatter_table(own[s : s + 1, :], own[4 + s : 5 + s, :], first, count, iota, "all")
    at = pl.ds(where, count)
    n_ref[index, :, at, 0:8, :] = n.reshape(18, count, 8, 128)
    s_ref[index, :, at, 0:8, :] = p.reshape(18, count, 8, 128)
    above = scatter_table(up[s : s + 1, :], up[4 + s : 5 + s, :], first, count, iota, "low")
    below = scatter_table(down[s : s + 1, :], down[4 + s : 5 + s, :], first, count, iota, "high")
    shape = (9 * count, 8, 128)
    low = low_half(shape)
    for ref, a, b in zip((n_ref, s_ref), above, below):
        a, b = a.reshape(shape), b.reshape(shape)
        even = jnp.where(low, a, b)
        odd = pltpu.roll(jnp.where(low, b, a), 4, 1)
        halo = jnp.stack([even, odd], axis=1).reshape(18, count, 8, 128)
        ref[index, :, at, 8:16, :] = halo


def read_list(ref, start):
    return jnp.concatenate([ref[start + t] for t in range(8)], axis=1)


def own_links_kernel(lists, n_ref, s_ref):
    iota = iota256()
    three = [lists[8 * k : 8 * k + 8, :] for k in range(3)]
    for s in range(4):
        scatter_columns(three, s, s, 0, 4, iota, n_ref, s_ref, 0)


def side_links_kernel(from_left, from_right, n_ref, s_ref):
    iota = iota256()
    for side, ref in enumerate((from_left, from_right)):
        three = [ref[8 * k : 8 * k + 8, :] for k in range(3)]
        for s in range(4):
            count = SIDE_COUNT[s]
            first = 0 if side else 4 - count
            scatter_columns(three, s, side, first, count, iota, n_ref, s_ref, SIDE_BASE[s])


def column_groups(s, n_own, s_own, n_side, s_side):
    count, base = SIDE_COUNT[s], SIDE_BASE[s]
    return (
        (4 - count, count, lambda q, i: n_side[0, q, base + i], lambda q, i: s_side[0, q, base + i]),
        (4, 4, lambda q, i: n_own[s, q, i], lambda q, i: s_own[s, q, i]),
        (8, count, lambda q, i: n_side[1, q, base + i], lambda q, i: s_side[1, q, base + i]),
    )


def shifted(value, cy, cz):
    if cy:
        value = pltpu.roll(value, cy % 16, 0)
    if cz:
        value = pltpu.roll(value, cz % 128, 1)
    return value


def moments(f):
    rho = f[0]
    for q in range(1, 19):
        rho = rho + f[q]
    inverse = 1.0 / rho
    speeds = []
    for c in range(3):
        total = None
        for q in range(1, 19):
            v = VELOCITIES[q][c]
            if v:
                total = (f[q] if v > 0 else -f[q]) if total is None else (total + f[q] if v > 0 else total - f[q])
        speeds.append(total * inverse)
    return rho, speeds


def along(speeds, q):
    total = None
    for c in range(3):
        v = VELOCITIES[q][c]
        if v:
            term = speeds[c] if v > 0 else -speeds[c]
            total = term if total is None else total + term
    return total


def collide_column(f):
    rho, speeds = moments(f)
    rest = 1.0 - 1.5 * (speeds[0] * speeds[0] + speeds[1] * speeds[1] + speeds[2] * speeds[2])
    out = [(1.0 - OMEGA) * f[0] + (OMEGA * WEIGHTS[0]) * rho * rest]
    for q in range(1, 19, 2):
        cu = along(speeds, q)
        scale = (OMEGA * WEIGHTS[q]) * rho
        even = scale * (rest + 4.5 * cu * cu)
        odd = scale * (3.0 * cu)
        out.append((1.0 - OMEGA) * f[q] + (even + odd))
        out.append((1.0 - OMEGA) * f[q + 1] + (even - odd))
    return out, rho


def collide_into(load, start, count, relaxed, density):
    def body(i, carry):
        f = [load(q, i) for q in range(19)]
        g, rho = collide_column(f)
        for q in range(19):
            relaxed[q, start + i] = g[q]
        density[start + i] = rho
        return carry

    lax.fori_loop(0, count, body, 0)


def stream_into(relaxed, density, groups, out):
    for start, count, counts, pushes in groups:

        def body(i, carry):
            x = start + i
            rho = density[x]
            out[0, x] = relaxed[0, x]
            for q in range(1, 19):
                p = OPPOSITE[q]
                cx, cy, cz = VELOCITIES[q]
                moved = shifted(relaxed[q, x - cx], cy, cz)
                bounce = (0.5 * counts(q - 1, i)) * (relaxed[p, x] - relaxed[q, x])
                push = (6.0 * WEIGHTS[q]) * rho * pushes(q - 1, i)
                out[q, x] = moved + (bounce - push)
            return carry

        lax.fori_loop(0, count, body, 0)


def adjoint_column(f, arrived, local, counts, pushes):
    rho, speeds = moments(f)
    b = [arrived[0]]
    direct = None
    for q in range(1, 19):
        p = OPPOSITE[q]
        b.append(
            arrived[q] + 0.5 * (counts[p - 1] * local[p] - counts[q - 1] * local[q])
        )
        term = (6.0 * WEIGHTS[q]) * (pushes[q - 1] * local[q])
        direct = term if direct is None else direct + term
    beta = [WEIGHTS[q] * b[q] for q in range(19)]
    total = beta[0]
    first = [None] * 3
    second = [None] * 3
    for q in range(1, 19, 2):
        plus = beta[q] + beta[q + 1]
        minus = beta[q] - beta[q + 1]
        total = total + plus
        inner = along(speeds, q) * plus
        for c in range(3):
            v = VELOCITIES[q][c]
            if v:
                m = minus if v > 0 else -minus
                k = inner if v > 0 else -inner
                first[c] = m if first[c] is None else first[c] + m
                second[c] = k if second[c] is None else second[c] + k
    square = speeds[0] * speeds[0] + speeds[1] * speeds[1] + speeds[2] * speeds[2]
    curved = speeds[0] * second[0] + speeds[1] * second[1] + speeds[2] * second[2]
    rest = OMEGA * (total - 4.5 * curved + 1.5 * square * total) - direct
    slopes = [
        OMEGA * (3.0 * first[c] + 9.0 * second[c] - 3.0 * speeds[c] * total) for c in range(3)
    ]
    out = [(1.0 - OMEGA) * b[0] + rest]
    for q in range(1, 19, 2):
        cu = along(slopes, q)
        out.append((1.0 - OMEGA) * b[q] + (rest + cu))
        out.append((1.0 - OMEGA) * b[q + 1] + (rest - cu))
    return out, rho


def adjoint_at(load_f, adjoint, x, counts, pushes):
    f = [load_f(q) for q in range(19)]
    local = [adjoint(q, x) for q in range(19)]
    arrived = []
    for q in range(19):
        cx, cy, cz = VELOCITIES[q]
        value = adjoint(q, x + cx) if cx else local[q]
        arrived.append(shifted(value, -cy, -cz))
    out, rho = adjoint_column(
        f, arrived, local, [counts(q) for q in range(18)], [pushes(q) for q in range(18)]
    )
    return out, rho, local


def ext(ref, k):
    return jnp.concatenate([ref[k], ref[k + 1]], axis=0)


def window_kernel(
    pops,
    seed,
    from_up,
    from_down,
    left_hbm,
    right_hbm,
    n_own,
    s_own,
    n_side,
    s_side,
    f1_out,
    a2_out,
    up_msg,
    down_msg,
    pull,
    relaxed,
    density,
    f2,
    f3,
    a4,
    a3,
    own_pops,
    from_left,
    from_right,
    sems,
):
    def groups(s):
        return column_groups(s, n_own, s_own, n_side, s_side)

    copies = [
        pltpu.make_async_copy(left_hbm, from_left, sems.at[0]),
        pltpu.make_async_copy(right_hbm, from_right, sems.at[1]),
    ]
    for copy in copies:
        copy.start()
    low = low_half((8, 128))
    for kind, q, x, own, halo in extended(pops, seed, from_up, from_down, low, row_iota((8, 128))):
        if kind == 0:
            own_pops[(q * 4 + x) * 2] = own
            own_pops[(q * 4 + x) * 2 + 1] = halo
        else:
            a4[q, 4 + x, 0:8] = own
            a4[q, 4 + x, 8:16] = halo
    for ref, start, count in ((own_pops, 4, 4), (from_left, 1, 3), (from_right, 8, 3)):
        if start == 1:
            for copy in copies:
                copy.wait()

        def load(q, i, ref=ref, count=count):
            return ref[pl.ds((q * count + i) * 2, 2)].reshape(16, 128)

        collide_into(load, start, count, relaxed, density)
    for i in range(5):
        relaxed[OUTWARD[1][i], 0] = ext(from_left, FAR_POPS + 2 * i)
        relaxed[OUTWARD[0][i], 11] = ext(from_right, FAR_POPS + 2 * i)
    stream_into(relaxed, density, groups(0), f2)
    for q in range(19):
        f1_out[q] = f2[q, 3:9]
    collide_into(lambda q, i: f2[q, 1 + i], 1, 10, relaxed, density)
    stream_into(relaxed, density, groups(1), f2)
    collide_into(lambda q, i: f2[q, 2 + i], 2, 8, relaxed, density)
    stream_into(relaxed, density, groups(2), f3)
    for q in range(19):
        a4[q, 3] = ext(from_left, NEAR_SEED + 2 * q)
        a4[q, 8] = ext(from_right, NEAR_SEED + 2 * q)
    for i in range(5):
        a4[OUTWARD[0][i], 2] = ext(from_left, FAR_SEED + 2 * i)
        a4[OUTWARD[1][i], 9] = ext(from_right, FAR_SEED + 2 * i)
    for start, count, counts, pushes in groups(3):

        def third(i, carry, start=start, count=count, counts=counts, pushes=pushes):
            x = start + i
            out, rho, local = adjoint_at(
                lambda q: f3[q, x],
                lambda q, at: a4[q, at],
                x,
                lambda q: counts(q, i),
                lambda q: pushes(q, i),
            )
            for q in range(19):
                a3[q, x] = out[q]
            if count == 4:
                for q in range(1, 19):
                    pull[0, q - 1, i] = ((-6.0 * WEIGHTS[q]) * rho * local[q])[:8]
            return carry

        lax.fori_loop(0, count, third, 0)

    def second(i, carry):
        x = 4 + i
        out, rho, local = adjoint_at(
            lambda q: f2[q, x],
            lambda q, at: a3[q, at],
            x,
            lambda q: n_own[2, q, i],
            lambda q: s_own[2, q, i],
        )
        rho1 = f1_out[0, 1 + i]
        for q in range(1, 19):
            rho1 = rho1 + f1_out[q, 1 + i]
        for q in range(19):
            a2_out[q, i] = out[q][:8]
        for q in range(1, 19):
            pull[1, q - 1, i] = ((-6.0 * WEIGHTS[q]) * rho * local[q])[:8]
            pull[2, q - 1, i] = ((-6.0 * WEIGHTS[q]) * rho1 * out[q])[:8]
        return carry

    lax.fori_loop(0, 4, second, 0)
    pair = row_iota((8, 128)) // 2
    for q in range(19):
        down_msg[q], up_msg[q] = edge_rows([a2_out[q, x] for x in range(4)], pair)


A_TILES = 48


def pack_adjoint_kernel(a2, from_up, from_down, right_msg, left_msg, middle):
    sub = row_iota((8, 128))
    for q in range(19):
        for x in range(4):
            own, halo = a2[q, x], widen_two(from_up[q], from_down[q], x, sub)
            if x in (0, 3):
                msg, k = (left_msg if x == 0 else right_msg), 2 * q
            else:
                msg, k = middle, (q * 2 + x - 1) * 2
            msg[k] = own
            msg[k + 1] = halo
            for side, edge in ((right_msg, 0), (left_msg, 1)):
                if x == 2 - edge and q in OUTWARD[edge]:
                    k = 38 + 2 * OUTWARD[edge].index(q)
                    side[k] = own
                    side[k + 1] = halo


def link_gradient(pulls, lists, steps):
    iota = iota256()
    total = jnp.zeros((32, 192), F32)
    lanes = row_iota((128, 1024))
    for i, s in enumerate(steps):
        code = lists[s : s + 1, :]
        dead, lane_q, x, y, z = split_code(code)
        row = jnp.where(dead, -1, lane_q * 32 + x * 8 + y).astype(F32)
        hot = onehot(row, 576, iota)
        high = pulls[i].astype(BF16)
        rest = (pulls[i] - high.astype(F32)).astype(BF16)
        low = (pulls[i] - high.astype(F32) - rest.astype(F32)).astype(BF16)
        picked = lax.dot_general(
            jnp.concatenate([high, rest, low], axis=1),
            hot,
            (((0,), (0,)), ((), ())),
            preferred_element_type=F32,
        )
        match = lanes == z
        value = jnp.sum(
            jnp.where(match, picked[:128] + picked[128:256] + picked[256:], 0.0),
            axis=0,
            keepdims=True,
        )
        slot = lists[4 + s : 5 + s, :].astype(jnp.int32)
        opposite = code.astype(jnp.int32) // 4096
        owner = onehot((slot // 64).astype(F32), 32, iota)
        place = row_iota((64, 1024)) == slot % 64
        parts = jnp.concatenate(
            [jnp.where(place, -value * signs(opposite, c), 0.0) for c in range(3)], axis=0
        )
        high = parts.astype(BF16)
        rest = (parts - high.astype(F32)).astype(BF16)
        low = (parts - high.astype(F32) - rest.astype(F32)).astype(BF16)
        summed = lax.dot_general(
            owner,
            jnp.concatenate([high, rest, low], axis=0),
            (((1,), (1,)), ((), ())),
            preferred_element_type=F32,
        )
        total = total + (summed[:, :192] + summed[:, 192:384] + summed[:, 384:])
    return total


def late_links_kernel(pull, lists, out):
    pulls = [pull[i].reshape(576, 128) for i in range(2)]
    out[...] = link_gradient(pulls, lists, (3, 2))


def early_links_kernel(pull, lists, late, out):
    out[...] = late[...] + link_gradient([pull[2].reshape(576, 128)], lists, (1,))


def first_adjoint_kernel(
    right_msg,
    left_msg,
    middle,
    from_left,
    from_right,
    pops,
    f1,
    n_own,
    s_own,
    n_side,
    s_side,
    late,
    lists,
    a1_out,
    grad_out,
    a1,
    a2,
    pull,
    sem,
):
    for q in range(19):
        a2[q, 1] = ext(from_left, 2 * q)
        a2[q, 2] = ext(left_msg, 2 * q)
        a2[q, 3] = ext(middle, 4 * q)
        a2[q, 4] = ext(middle, 4 * q + 2)
        a2[q, 5] = ext(right_msg, 2 * q)
        a2[q, 6] = ext(from_right, 2 * q)
    for i in range(5):
        a2[OUTWARD[0][i], 0] = ext(from_left, 38 + 2 * i)
        a2[OUTWARD[1][i], 7] = ext(from_right, 38 + 2 * i)
    left, own, right = column_groups(1, n_own, s_own, n_side, s_side)
    for at, count, group, skip in ((0, 1, left, 1), (1, 4, own, 0), (5, 1, right, 0)):

        def first(i, carry, at=at, count=count, group=group, skip=skip):
            out, rho, local = adjoint_at(
                lambda q: f1[q, at + i],
                lambda q, x: a2[q, x],
                at + i + 1,
                lambda q: group[2](q, i + skip),
                lambda q: group[3](q, i + skip),
            )
            for q in range(19):
                a1[q, at + i] = out[q]
            if count == 4:
                rho0 = pops[0, i]
                for q in range(1, 19):
                    rho0 = rho0 + pops[q, i]
                for q in range(1, 19):
                    pull[q - 1, i] = (-6.0 * WEIGHTS[q]) * rho0 * out[q][:8]
            return carry

        lax.fori_loop(0, count, first, 0)
    copy = pltpu.make_async_copy(a1, a1_out, sem.at[0])
    copy.start()
    total = late[...] + link_gradient([pull[...].reshape(576, 128)], lists, (0,))
    grad_out[...] = total.reshape(32, 1, 192)
    copy.wait()


def total_kernel(parts, out):
    total = parts[0]
    for k in range(1, 32):
        total = total + parts[k]
    for c in range(3):
        out[c : c + 1, :] = total[:, 64 * c : 64 * c + 64]


def last_adjoint_kernel(a1, pops, n_own, s_own, a0_out):
    def last(i, carry):
        f = [pops[q, i] for q in range(19)]
        local = [a1[q, 1 + i] for q in range(19)]
        arrived = []
        for q in range(19):
            cx, cy, cz = VELOCITIES[q]
            value = a1[q, 1 + i + cx] if cx else local[q]
            arrived.append(shifted(value, -cy, -cz)[:8])
        local = [v[:8] for v in local]
        out, _ = adjoint_column(
            f,
            arrived,
            local,
            [n_own[0, q, i, 0:8] for q in range(18)],
            [s_own[0, q, i, 0:8] for q in range(18)],
        )
        for q in range(19):
            a0_out[q, i] = out[q]
        return carry

    lax.fori_loop(0, 4, last, 0)


def ring(axis, step):
    count = lax.axis_size(axis)
    return [(i, (i + step) % count) for i in range(count)]


def shape(*dims, dtype=F32):
    return jax.ShapeDtypeStruct(dims, dtype)


def cost(flops, bytes_accessed):
    return pl.CostEstimate(flops=flops, bytes_accessed=bytes_accessed, transcendentals=0)


def call(kernel, name, out_shape, count, limit, scratch=(), smem=0, flops=0, moved=0):
    vmem = full()
    many = isinstance(out_shape, list)
    return pl.pallas_call(
        kernel,
        name=name,
        out_shape=out_shape,
        in_specs=[pl.BlockSpec(memory_space=pltpu.SMEM)] * smem + [vmem] * (count - smem),
        out_specs=[vmem] * len(out_shape) if many else vmem,
        scratch_shapes=list(scratch),
        cost_estimate=cost(flops, moved) if flops else None,
        compiler_params=pltpu.CompilerParams(vmem_limit_bytes=limit << 20),
    )


def shards(
    populations, wall_speed, adjoint_seed, link_cell, link_dir, link_node, live_links, node_slot
):
    base = (lax.axis_index("gx") * 2048).astype(jnp.int32).reshape(1)
    smem = pl.BlockSpec(memory_space=pltpu.SMEM)
    operands = (
        populations,
        adjoint_seed,
        wall_speed,
        link_cell,
        link_dir,
        link_node,
        node_slot.reshape(128, 128),
    )
    up_msg, down_msg, lists, copies, pops, seed = pl.pallas_call(
        front_kernel,
        name="front",
        out_shape=[
            shape(Y_TILES, 8, 128),
            shape(Y_TILES, 8, 128),
            shape(8, 1024),
            shape(32, 1, 192),
            shape(19, 4, 8, 128),
            shape(19, 4, 8, 128),
        ],
        in_specs=[smem] + [pl.BlockSpec(memory_space=pltpu.HBM)] * 8,
        out_specs=[full()] * 6,
        scratch_shapes=[pltpu.VMEM(a.shape, a.dtype) for a in operands[2:]]
        + [pltpu.SMEM((4,), jnp.int32), pltpu.SemaphoreType.DMA((8,))],
        compiler_params=pltpu.CompilerParams(vmem_limit_bytes=12 << 20),
    )(
        base,
        *(
            pltpu.with_memory_space_constraint(a, pltpu.HBM)
            for a in (live_links.reshape(4), *operands)
        ),
    )
    from_down = lax.ppermute(up_msg, "gy", ring("gy", 1))
    from_up = lax.ppermute(down_msg, "gy", ring("gy", -1))
    wall = lax.all_to_all(copies, "gy", split_axis=0, concat_axis=0, tiled=True)
    right_msg, left_msg = call(
        pack_kernel,
        "pack",
        [shape(X_TILES, 8, 128)] * 2,
        4,
        8,
        [pltpu.VMEM((SEED_TILES, 8, 128), F32)],
    )(pops, seed, from_up, from_down)
    lists, right_msg, left_msg = lax.optimization_barrier((lists, right_msg, left_msg))
    from_left = lax.ppermute(right_msg, "gx", ring("gx", 1))
    from_right = lax.ppermute(left_msg, "gx", ring("gx", -1))
    all_lists = call(push_kernel, "push", shape(24, 1024), 4, 8, flops=500_000_000, moved=500_000)(
        wall, lists, from_up, from_down
    )
    left_lists = lax.ppermute(all_lists, "gx", ring("gx", 1))
    right_lists = lax.ppermute(all_lists, "gx", ring("gx", -1))
    n_own, s_own = call(
        own_links_kernel,
        "own_links",
        [shape(4, 18, 4, 16, 128)] * 2,
        1,
        24,
        flops=3_500_000_000,
        moved=1_000_000,
    )(all_lists)
    n_side, s_side = call(
        side_links_kernel,
        "side_links",
        [shape(2, 18, 7, 16, 128)] * 2,
        2,
        24,
        flops=3_500_000_000,
        moved=1_000_000,
    )(left_lists, right_lists)
    region = pltpu.VMEM((19, 12, 16, 128), F32)
    arrived = pltpu.VMEM((X_TILES, 8, 128), F32)
    f1, a2, up_msg, down_msg, pull = pl.pallas_call(
        window_kernel,
        name="window",
        out_shape=[
            shape(19, 6, 16, 128),
            shape(19, 4, 8, 128),
            shape(19, 8, 128),
            shape(19, 8, 128),
            shape(3, 18, 4, 8, 128),
        ],
        in_specs=[full()] * 4 + [pl.BlockSpec(memory_space=pl.ANY)] * 2 + [full()] * 4,
        out_specs=[full()] * 5,
        scratch_shapes=[region, pltpu.VMEM((12, 16, 128), F32), region, region, region, region]
        + [pltpu.VMEM((POP_TILES, 8, 128), F32), arrived, arrived, pltpu.SemaphoreType.DMA((2,))],
        compiler_params=pltpu.CompilerParams(vmem_limit_bytes=32 << 20),
    )(pops, seed, from_up, from_down, from_left, from_right, n_own, s_own, n_side, s_side)
    from_down = lax.ppermute(up_msg, "gy", ring("gy", 1))
    from_up = lax.ppermute(down_msg, "gy", ring("gy", -1))
    late = call(
        late_links_kernel, "late_links", shape(32, 192), 2, 16, flops=2_000_000_000, moved=2_000_000
    )(pull, lists)
    late, from_up, from_down = lax.optimization_barrier((late, from_up, from_down))
    right_msg, left_msg, middle = call(
        pack_adjoint_kernel,
        "pack_adjoint",
        [shape(A_TILES, 8, 128), shape(A_TILES, 8, 128), shape(SEED_TILES, 8, 128)],
        3,
        4,
    )(a2, from_up, from_down)
    from_left = lax.ppermute(right_msg, "gx", ring("gx", 1))
    from_right = lax.ppermute(left_msg, "gx", ring("gx", -1))
    late = call(
        early_links_kernel,
        "early_links",
        shape(32, 192),
        3,
        16,
        flops=1_000_000_000,
        moved=1_000_000,
    )(pull, lists, late)
    a1, owned = pl.pallas_call(
        first_adjoint_kernel,
        name="first_adjoint",
        out_shape=[pltpu.HBM((19, 6, 16, 128), F32), shape(32, 1, 192)],
        in_specs=[full()] * 13,
        out_specs=[pl.BlockSpec(memory_space=pltpu.HBM), full()],
        scratch_shapes=[
            pltpu.VMEM((19, 6, 16, 128), F32),
            pltpu.VMEM((19, 8, 16, 128), F32),
            pltpu.VMEM((18, 4, 8, 128), F32),
            pltpu.SemaphoreType.DMA((1,)),
        ],
        compiler_params=pltpu.CompilerParams(vmem_limit_bytes=24 << 20),
    )(
        right_msg,
        left_msg,
        middle,
        from_left,
        from_right,
        pops,
        f1,
        n_own,
        s_own,
        n_side,
        s_side,
        late,
        lists,
    )
    arrived = lax.all_to_all(owned, "gy", split_axis=0, concat_axis=0, tiled=True)
    adjoint = call(
        last_adjoint_kernel,
        "last_adjoint",
        shape(19, 4, 8, 128),
        4,
        12,
        flops=10_000_000,
        moved=4_000_000,
    )(a1, pops, n_own, s_own)
    gradient = call(total_kernel, "total", shape(3, 64), 1, 4)(arrived)
    return (adjoint, gradient)


def solution(mesh):
    placed = (
        P(None, "gx", "gy", None),
        P(None, ("gx", "gy")),
        P(None, "gx", "gy", None),
        P(None, ("gx", "gy")),
        P(None, ("gx", "gy")),
        P(None, ("gx", "gy")),
        P(None, ("gx", "gy")),
        P(),
    )
    return jax.shard_map(
        shards,
        mesh=mesh,
        in_specs=placed,
        out_specs=(P(None, "gx", "gy", None), P(None, ("gx", "gy"))),
        check_vma=False,
    )
```
